32 devices in a mesh: dp: 16 (over z, x, core), mp: 2 (over y).
Axes of the slice: x: 2, y: 2, z: 4, core: 2. Of those that a mesh axis runs over, the one named last changes fastest.
Arguments:
- inputs: bfloat16 [2048, 2048], P('dp'), may hold values from -6 to 6
- segments: int32 [16, 128], P('dp'), may hold values from 0 to 1, never falling along the last dimension, each value on 1 to 96 neighbouring positions
- example_of: int32 [16, 2], P('dp'), may hold values from 0 to 1, each once within a row
- patches: bfloat16 [32, 64, 2048], P('dp'), may hold values from -6 to 6
- grad_out: bfloat16 [2048, 2048], P('dp'), may hold values from -6 to 6
- gain_self: bfloat16 [2048], P('dp'), may hold values from 0.5 to 1.5
- wq_self: bfloat16 [2048, 2048], P('dp', 'mp'), may hold values from -0.25 to 0.25
- wk_self: bfloat16 [2048, 2048], P('dp', 'mp'), may hold values from -0.125 to 0.125
- wv_self: bfloat16 [2048, 2048], P('dp', 'mp'), may hold values from -0.125 to 0.125
- wo_self: bfloat16 [2048, 2048], P('mp', 'dp'), may hold values from -0.25 to 0.25
- gain_cross: bfloat16 [2048], P('dp'), may hold values from 0.5 to 1.5
- wq_cross: bfloat16 [2048, 2048], P('dp', 'mp'), may hold values from -0.25 to 0.25
- wk_cross: bfloat16 [2048, 2048], P('dp', 'mp'), may hold values from -0.125 to 0.125
- wv_cross: bfloat16 [2048, 2048], P('dp', 'mp'), may hold values from -0.125 to 0.125
- wo_cross: bfloat16 [2048, 2048], P('mp', 'dp'), may hold values from -0.25 to 0.25
- gain_ffn: bfloat16 [2048], P('dp'), may hold values from 0.5 to 1.5
- w_gate: bfloat16 [2048, 5120], P('dp', 'mp'), may hold values from -0.125 to 0.125
- w_up: bfloat16 [2048, 5120], P('dp', 'mp'), may hold values from -0.125 to 0.125
- w_down: bfloat16 [5120, 2048], P('mp', 'dp'), may hold values from -0.078125 to 0.078125
Outputs:
- output: float32 [2048, 2048], P('dp')
- grad_inputs: float32 [2048, 2048], P('dp')
- grad_patches: float32 [32, 64, 2048], P('dp')
- grad_gain_self: float32 [2048], P('dp')
- grad_wq_self: float32 [2048, 2048], P('dp', 'mp')
- grad_wk_self: float32 [2048, 2048], P('dp', 'mp')
- grad_wv_self: float32 [2048, 2048], P('dp', 'mp')
- grad_wo_self: float32 [2048, 2048], P('mp', 'dp')
- grad_gain_cross: float32 [2048], P('dp')
- grad_wq_cross: float32 [2048, 2048], P('dp', 'mp')
- grad_wk_cross: float32 [2048, 2048], P('dp', 'mp')
- grad_wv_cross: float32 [2048, 2048], P('dp', 'mp')
- grad_wo_cross: float32 [2048, 2048], P('mp', 'dp')
- grad_gain_ffn: float32 [2048], P('dp')
- grad_w_gate: float32 [2048, 5120], P('dp', 'mp')
- grad_w_up: float32 [2048, 5120], P('dp', 'mp')
- grad_w_down: float32 [5120, 2048], P('mp', 'dp')
The draws below stay inside these ranges and needn't reach their ends.
Inputs may be any that keep to these rules, and one draw needn't show every extreme that they name: In each row the segment numbers never fall and each of the 2 segments holds at least one token. `example_of`: each row holds every number below 2 once.
All inputs are finite; a program needn't handle non-finite values.
Results may differ from the reference program's by a relative error of at most 0.025.
The reference program's roundings to bfloat16 on the way count: a program that leaves them out, or rounds other values in their place, can miss the bound.
Values may be sent and summed in bfloat16 or wider, within the bound.
No kernel may reach another device: no remote copies, remote signals or barrier semaphores. Data moves between devices by JAX's collectives and lax.ppermute only.
A program may use at most 320 MiB of HBM per device.

```python
import math
from functools import partial
import jax
import jax.numpy as jnp
import numpy as np
from jax import lax

D = 2048
HEADS = 32
HEAD_DIM = 64
FF = 5120
PATCHES = 64
ROW_LEN = 128
SEGS = 2
EX_DEV = 2
BLOCKS = 16
ROWS = 16
TOKENS = 2048
EXAMPLES = 32


def with_spikes(drawn, rng, source, target, parts, factor):
    def block_of(dim):
        return (jnp.arange(drawn.shape[dim]) // (drawn.shape[dim] // parts)).reshape((-1,) + (1,) * (drawn.ndim - 1 - dim))

    near = jax.random.permutation(rng, parts)[block_of(target)]
    other_side = (block_of(target) + parts // 2) % parts
    return jnp.where((block_of(source) == near) | (block_of(source) == other_side), factor * drawn, drawn)


def block_levels(key, extent, cuts, low, top_value):
    level, own = 1.0, jax.random.fold_in(key, 6)
    for dim, shards_of in cuts:
        draws = jnp.exp(jax.random.uniform(jax.random.fold_in(own, dim), (shards_of,), jnp.float32, low / len(cuts), top_value / len(cuts)))
        level = level * jnp.repeat(draws, extent[dim] // shards_of).reshape([-1 if axis == dim else 1 for axis in range(len(extent))])
    return level


def length_profile(amount, total, limit, slope):
    weights = [(1 << 20) // math.isqrt(grade ** slope) + 1 for grade in range(2, amount + 1)]
    spare, holding = total - limit - (amount - 1), [1] * (amount - 1)
    while spare > 0:
        movable = [i for i in range(amount - 1) if holding[i] < limit]
        mass, remaining = sum([weights[i] for i in movable]), spare
        for i in movable:
            more = min(limit - holding[i], max(1, remaining * weights[i] // mass), spare)
            holding[i] = holding[i] + more
            spare = spare - more
    return np.array([limit] + holding)


def ragged(key, count, total, reach, lean):
    if count == 2:
        one = jax.random.randint(key, (), max(1, total - reach), min(reach, total - 1) + 1)
        return jnp.stack([one, total - one])
    sizes = jnp.asarray(length_profile(count, total, reach, lean), jnp.int32)
    pairs = (count - 1) // 2
    source_of, taker = sizes[1:1 + 2 * pairs:2], sizes[2:2 + 2 * pairs:2]
    room = jnp.minimum(source_of - 1, reach - taker)
    shifted = jax.random.randint(jax.random.fold_in(key, 1), (pairs,), 0, 1 << 20) % (room + 1)
    sizes = sizes.at[1:1 + 2 * pairs:2].set(source_of - shifted).at[2:2 + 2 * pairs:2].set(taker + shifted)
    return sizes[jax.random.permutation(jax.random.fold_in(key, 2), count)]


def gaussian(own_key, extent, spread, most, pieces=(), kind=jnp.bfloat16):
    values = jax.random.normal(own_key, extent, jnp.float32) * spread
    if len(pieces) > 0:
        values = block_levels(own_key, extent, pieces, -0.22, 0.18) * values
    return jnp.clip(values, min=-most, max=most).astype(kind)


def noise_with(rng, extent, spread, most, pieces, heavy, held_as=jnp.bfloat16):
    entries = spread * jax.random.normal(rng, extent, jnp.float32)
    if pieces:
        entries = entries * block_levels(rng, extent, pieces, -0.22, 0.18)
    return jnp.clip(with_spikes(entries, jax.random.fold_in(rng, 3), *heavy), -most, most).astype(held_as)


def setup_inputs(seed: int = 0) -> dict:
    key_of = jax.random.split(jax.random.key(seed), 20)
    return {
        "inputs": noise_with(key_of[0], (TOKENS, D), 1.0, 6.0, ((0, 16),), (0, 1, 16, 2.0)),
        "segments": jax.vmap(lambda own: jnp.searchsorted(jnp.cumsum(ragged(own, SEGS, ROW_LEN, ROW_LEN * 3 // 4, 0)), jnp.arange(ROW_LEN), side="right"))(jax.random.split(key_of[1], ROWS)).reshape((ROWS, ROW_LEN)).astype(jnp.int32),
        "example_of": jax.vmap(lambda own: jax.random.permutation(own, EX_DEV))(jax.random.split(key_of[2], BLOCKS)).reshape((BLOCKS, EX_DEV)).astype(jnp.int32),
        "patches": gaussian(key_of[3], (EXAMPLES, PATCHES, D), 1.0, 6.0, ((0, 16),)),
        "grad_out": noise_with(key_of[4], (TOKENS, D), 1.0, 6.0, ((0, 16),), (0, 1, 16, 2.0)),
        "gain_self": jnp.clip(1.0 + 0.1 * jax.random.normal(key_of[5], (D,), jnp.float32), 0.5, 1.5).astype(jnp.bfloat16),
        "wq_self": gaussian(key_of[6], (D, HEADS * HEAD_DIM), (D // 4) ** -0.5, 0.25, ((0, 16), (1, 2))),
        "wk_self": gaussian(key_of[7], (D, HEADS * HEAD_DIM), D ** -0.5, 0.125, ((0, 16), (1, 2))),
        "wv_self": gaussian(key_of[8], (D, HEADS * HEAD_DIM), D ** -0.5, 0.125, ((0, 16), (1, 2))),
        "wo_self": gaussian(key_of[9], (HEADS * HEAD_DIM, D), (HEADS * HEAD_DIM // 4) ** -0.5, 0.25, ((0, 2), (1, 16))),
        "gain_cross": jnp.clip(1.0 + 0.1 * jax.random.normal(key_of[10], (D,), jnp.float32), 0.5, 1.5).astype(jnp.bfloat16),
        "wq_cross": gaussian(key_of[11], (D, HEADS * HEAD_DIM), (D // 4) ** -0.5, 0.25, ((0, 16), (1, 2))),
        "wk_cross": gaussian(key_of[12], (D, HEADS * HEAD_DIM), D ** -0.5, 0.125, ((0, 16), (1, 2))),
        "wv_cross": gaussian(key_of[13], (D, HEADS * HEAD_DIM), D ** -0.5, 0.125, ((0, 16), (1, 2))),
        "wo_cross": gaussian(key_of[14], (HEADS * HEAD_DIM, D), (HEADS * HEAD_DIM // 4) ** -0.5, 0.25, ((0, 2), (1, 16))),
        "gain_ffn": jnp.clip(1.0 + 0.1 * jax.random.normal(key_of[15], (D,), jnp.float32), 0.5, 1.5).astype(jnp.bfloat16),
        "w_gate": gaussian(key_of[16], (D, FF), D ** -0.5, 0.125, ((0, 16), (1, 2))),
        "w_up": gaussian(key_of[17], (D, FF), D ** -0.5, 0.125, ((0, 16), (1, 2))),
        "w_down": gaussian(key_of[18], (FF, D), FF ** -0.5, 0.078125, ((0, 2), (1, 16))),
    }


EPS = 1e-06
NEG = -1e+30

@jax.custom_vjp
def low(v):
    return lax.optimization_barrier(v.astype(jnp.bfloat16)).astype(jnp.float32)

@jax.custom_vjp
def low_back(v):
    return v

def low_keep(v):
    return (low(v), None)

def low_pass(kept, grad):
    return (grad,)

def back_keep(v):
    return (v, None)

def back_low(kept, grad):
    return (low(grad),)
low.defvjp(low_keep, low_pass)
low_back.defvjp(back_keep, back_low)

def rms_norm(values, gain_row):
    return values * lax.rsqrt(lax.optimization_barrier(jnp.mean(values * values, axis=-1, keepdims=True)) + EPS) * gain_row

def matmul(first_operand, second_operand):
    return jnp.dot(first_operand, second_operand, precision=lax.Precision.HIGHEST)

def project(source, weight):
    return low(low_back(matmul(source, weight)))

def split_heads(matrix):
    return matrix.reshape(matrix.shape[0], HEADS, HEAD_DIM)

def attention(queries, key_rows, value_rows, allowed):
    score_scale = HEAD_DIM ** (-0.5)
    scores = low_back(jnp.einsum('qhe,khe->hqk', queries, key_rows, precision=lax.Precision.HIGHEST) * score_scale)
    scores = jnp.where(allowed[None], scores, NEG)
    row_max = lax.optimization_barrier(jnp.max(scores, axis=-1, keepdims=True))
    raised = jnp.exp(scores - row_max)
    softmax_rows = low(raised / lax.optimization_barrier(jnp.sum(raised, axis=-1, keepdims=True)))
    attended = jnp.einsum('hqk,khe->qhe', softmax_rows, value_rows, precision=lax.Precision.HIGHEST)
    return low(low_back(attended.reshape(attended.shape[0], HEADS * HEAD_DIM)))

def one_row(params, row_input, seg_row, memory):
    gain_self, wq_self, wk_self, wv_self, wo_self, gain_cross, wq_cross, wk_cross, wv_cross, wo_cross, gain_ffn, w_gate, w_up, w_down = params
    length = row_input.shape[0]
    positions = jnp.arange(length, dtype=jnp.int32)
    allowed = (seg_row[:, None] == seg_row[None, :]) & (positions[:, None] >= positions[None, :])
    normed = low(rms_norm(row_input, gain_self))
    attended = attention(split_heads(project(normed, wq_self)), split_heads(project(normed, wk_self)), split_heads(project(normed, wv_self)), allowed)
    after_self = row_input + low_back(matmul(attended, wo_self))
    normed = low(rms_norm(after_self, gain_cross))
    slot_ids = jnp.arange(memory.shape[0], dtype=jnp.int32) // PATCHES
    allowed = seg_row[:, None] == slot_ids[None, :]
    attended = attention(split_heads(project(normed, wq_cross)), split_heads(project(memory, wk_cross)), split_heads(project(memory, wv_cross)), allowed)
    after_cross = after_self + low_back(matmul(attended, wo_cross))
    normed = low(rms_norm(after_cross, gain_ffn))
    gate_values = low_back(matmul(normed, w_gate))
    up_values = low_back(matmul(normed, w_up))
    hidden = low(jax.nn.gelu(gate_values, approximate=True) * up_values)
    return after_cross + low_back(matmul(hidden, w_down))

def reference(inputs, segments, example_of, patches, grad_out, gain_self, wq_self, wk_self, wv_self, wo_self, gain_cross, wq_cross, wk_cross, wv_cross, wo_cross, gain_ffn, w_gate, w_up, w_down):
    params = tuple((weight.astype(jnp.float32) for weight in (gain_self, wq_self, wk_self, wv_self, wo_self, gain_cross, wq_cross, wk_cross, wv_cross, wo_cross, gain_ffn, w_gate, w_up, w_down)))
    row_count, row_length = segments.shape
    feature_count = inputs.shape[1]
    blocks, per_block = example_of.shape
    slot_count = blocks * per_block // row_count
    owners = (jnp.arange(blocks, dtype=jnp.int32)[:, None] * per_block + example_of).reshape(row_count * slot_count).astype(jnp.int32)
    group_rows = math.gcd(row_count, 8)

    def run_group(weights_in, row_items):
        rows_in, segs_in, memory_in = row_items

        def single(row_input, seg_row, memory):
            return one_row(weights_in, row_input, seg_row, memory)
        return jax.vmap(single)(rows_in, segs_in, memory_in)
    checkpointed = jax.checkpoint(run_group)

    def forward(start_rows, patch_rows, weights_in):
        memory_rows = jnp.take(patch_rows, owners, axis=0).reshape(row_count // group_rows, group_rows, -1, feature_count)
        outputs = lax.map(partial(checkpointed, weights_in), (start_rows.reshape(row_count // group_rows, group_rows, row_length, feature_count), segments.reshape(row_count // group_rows, group_rows, row_length), memory_rows))
        return outputs.reshape(row_count * row_length, feature_count)
    output, pullback = jax.vjp(forward, inputs.astype(jnp.float32), patches.astype(jnp.float32), params)
    grad_inputs, grad_patches, grad_params = pullback(grad_out.astype(jnp.float32))
    return (output, grad_inputs, grad_patches, grad_params[0], grad_params[1], grad_params[2], grad_params[3], grad_params[4], grad_params[5], grad_params[6], grad_params[7], grad_params[8], grad_params[9], grad_params[10], grad_params[11], grad_params[12], grad_params[13])
```

```python
import functools

import jax
import jax.numpy as jnp
from jax import lax
from jax.experimental import pallas as pl
from jax.experimental.pallas import tpu as pltpu
from jax.sharding import PartitionSpec as P

HEAD_DIM = 64
INNER = 4
EPS = 1e-06
NEG = -1e30
BF = jnp.bfloat16
F32 = jnp.float32


def dot(a, b, da, db):
    return lax.dot_general(a, b, (((da,), (db,)), ((), ())), preferred_element_type=F32)


def mask_of(qid_ref, kid_ref, causal):
    allowed = qid_ref[...] == kid_ref[...]
    if causal:
        rows = lax.broadcasted_iota(jnp.int32, allowed.shape, 0)
        cols = lax.broadcasted_iota(jnp.int32, allowed.shape, 1)
        allowed = allowed & (rows >= cols)
    return allowed


def soft(q, k, allowed):
    scores = jnp.where(allowed, dot(q, k, 1, 1) * HEAD_DIM ** (-0.5), NEG)
    raised = jnp.exp(scores - jnp.max(scores, axis=-1, keepdims=True))
    return raised / jnp.sum(raised, axis=-1, keepdims=True)


def attend_kernel(causal, qid_ref, kid_ref, q_ref, k_ref, v_ref, out_ref):
    allowed = mask_of(qid_ref, kid_ref, causal)
    pieces = []
    for first in range(0, q_ref.shape[1], HEAD_DIM):
        cut = slice(first, first + HEAD_DIM)
        probs = soft(q_ref[:, cut], k_ref[:, cut], allowed).astype(BF)
        pieces.append(dot(probs, v_ref[:, cut], 1, 0).astype(BF))
    out_ref[...] = jnp.concatenate(pieces, axis=1)


def attend_back_kernel(causal, qid_ref, kid_ref, q_ref, k_ref, v_ref, g_ref, dq_ref, dkv_ref):
    allowed = mask_of(qid_ref, kid_ref, causal)
    scale = HEAD_DIM ** (-0.5)
    dqs, dks, dvs = [], [], []
    for first in range(0, q_ref.shape[1], HEAD_DIM):
        cut = slice(first, first + HEAD_DIM)
        q, k, v, g = q_ref[:, cut], k_ref[:, cut], v_ref[:, cut], g_ref[:, cut]
        probs = soft(q, k, allowed)
        grad_probs = dot(g, v, 1, 1)
        dvs.append(dot(probs.astype(BF), g, 0, 0).astype(BF))
        centre = jnp.sum(probs * grad_probs, axis=-1, keepdims=True)
        ds = (probs * (grad_probs - centre)).astype(BF)
        dqs.append((dot(ds, k, 1, 0) * scale).astype(BF))
        dks.append((dot(ds, q, 0, 0) * scale).astype(BF))
    dq_ref[...] = jnp.concatenate(dqs, axis=1)
    dkv_ref[...] = jnp.concatenate(dks + dvs, axis=1)


def id_specs(length, keys):
    return [
        pl.BlockSpec((None, length, 1), lambda r: (r, 0, 0)),
        pl.BlockSpec((None, 1, keys), lambda r: (r, 0, 0)),
    ]


def attend(causal, qid, kid, q, k, v):
    rows, length, _ = qid.shape
    keys = kid.shape[2]
    width = q[2]
    specs = [
        pl.BlockSpec((n, width), functools.partial(lambda c, r: (r, c), col))
        for n, col in ((length, q[1]), (keys, k[1]), (keys, v[1]))
    ]
    return pl.pallas_call(
        functools.partial(attend_kernel, causal),
        grid=(rows,),
        in_specs=id_specs(length, keys) + specs,
        out_specs=pl.BlockSpec((length, width), lambda r: (r, 0)),
        out_shape=jax.ShapeDtypeStruct((rows * length, width), BF),
        cost_estimate=pl.CostEstimate(
            flops=4 * rows * length * keys * width,
            transcendentals=rows * length * keys * width // HEAD_DIM,
            bytes_accessed=8 * rows * length * width,
        ),
    )(qid, kid, q[0], k[0], v[0])


def attend_back(causal, qid, kid, q, k, v, g):
    rows, length, _ = qid.shape
    keys = kid.shape[2]
    width = q[2]
    specs = [
        pl.BlockSpec((n, width), functools.partial(lambda c, r: (r, c), col))
        for n, col in ((length, q[1]), (keys, k[1]), (keys, v[1]), (length, 0))
    ]
    return pl.pallas_call(
        functools.partial(attend_back_kernel, causal),
        grid=(rows,),
        in_specs=id_specs(length, keys) + specs,
        out_specs=[
            pl.BlockSpec((length, width), lambda r: (r, 0)),
            pl.BlockSpec((keys, 2 * width), lambda r: (r, 0)),
        ],
        out_shape=[
            jax.ShapeDtypeStruct((rows * length, width), BF),
            jax.ShapeDtypeStruct((rows * keys, 2 * width), BF),
        ],
        cost_estimate=pl.CostEstimate(
            flops=10 * rows * length * keys * width,
            transcendentals=rows * length * keys * width // HEAD_DIM,
            bytes_accessed=14 * rows * length * width,
        ),
    )(qid, kid, q[0], k[0], v[0], g)


def rms(values, gain):
    scale = lax.rsqrt(jnp.mean(values * values, axis=-1, keepdims=True) + EPS)
    return (values * scale * gain).astype(BF), scale


def rms_back(values, scale, gain, grad):
    weighted = grad * gain
    mean = jnp.mean(weighted * values, axis=-1, keepdims=True)
    return (
        scale * weighted - values * (scale * scale * scale) * mean,
        jnp.sum(grad * values * scale, axis=0, keepdims=True),
    )


def gelu_parts(gate):
    c = (2.0 / jnp.pi) ** 0.5
    inner = jnp.tanh(c * (gate + 0.044715 * gate * gate * gate))
    value = 0.5 * gate * (1.0 + inner)
    slope = 0.5 * (1.0 + inner) + 0.5 * gate * (1.0 - inner * inner) * c * (
        1.0 + 3 * 0.044715 * gate * gate
    )
    return value, slope


def on_device(
    inputs,
    segments,
    example_of,
    patches,
    grad_out,
    gain_self,
    wq_self,
    wk_self,
    wv_self,
    wo_self,
    gain_cross,
    wq_cross,
    wk_cross,
    wv_cross,
    wo_cross,
    gain_ffn,
    w_gate,
    w_up,
    w_down,
):
    dp = lax.axis_size("dp")
    outer = dp // INNER
    place = lax.axis_index("dp")
    mine, plane = place % INNER, place // INNER
    odd, far = (mine & 1) == 1, (mine & 2) == 2
    tokens, width = inputs.shape
    part = width // dp
    block = INNER * part

    def swap(value, bit):
        return lax.ppermute(value, "dp", [(i, i ^ bit) for i in range(dp)])

    def swap_mp(value):
        return lax.ppermute(value, "mp", [(0, 1), (1, 0)])

    sent = []

    def hop(value):
        if len(sent) >= 2:
            value, _ = lax.optimization_barrier((value, sent[-2]))
        sent.append(lax.ppermute(value, "dp", [(i, (i + INNER) % dp) for i in range(dp)]))
        return sent[-1]

    def small_hop(value):
        return lax.ppermute(value, "dp", [(i, (i + INNER) % dp) for i in range(dp)])

    def natural(p0, p1, p2, p3):
        a0, a1 = jnp.where(odd, p1, p0), jnp.where(odd, p0, p1)
        a2, a3 = jnp.where(odd, p3, p2), jnp.where(odd, p2, p3)
        return (
            jnp.where(far, a2, a0),
            jnp.where(far, a3, a1),
            jnp.where(far, a0, a2),
            jnp.where(far, a1, a3),
        )

    def exchange(blocks):
        to = [lax.dynamic_index_in_dim(blocks, mine ^ j, 0, keepdims=False) for j in range(INNER)]
        first = swap(jnp.stack([to[2], to[3]]), 2)
        second = swap(jnp.stack([to[1], first[1]]), 1)
        return natural(to[0], second[0], first[0], second[1])

    def rows_of(value):
        away = swap(value, 2)
        near = swap(jnp.stack([value, away]), 1)
        return jnp.concatenate([value, near[0], away, near[1]], axis=0)

    def reduce_rows(partial):
        parts = partial.reshape(INNER, -1, partial.shape[1])
        near = swap(jnp.stack([parts[1], parts[3]]).astype(BF), 1).astype(F32)
        away = swap((parts[2] + near[1]).astype(BF), 2).astype(F32)
        total = (parts[0] + near[0] + away).astype(BF)
        return total.astype(F32) + swap_mp(total).astype(F32)

    def pack(weights):
        return jnp.stack(
            [
                jnp.concatenate(
                    [
                        w[:, i * (w.shape[1] // INNER) : (i + 1) * (w.shape[1] // INNER)]
                        for w in weights
                    ],
                    axis=1,
                )
                for i in range(INNER)
            ]
        )

    def gather_weights(weights):
        pieces = exchange(pack(weights))
        halves = [
            jnp.concatenate(pieces[:2], axis=0),
            jnp.concatenate(pieces[2:], axis=0),
        ]
        full = jnp.zeros((outer, 2, block // 2, halves[0].shape[1]), BF)
        held = halves
        for step in range(outer):
            if step:
                held = [hop(h) for h in held]
            where = (plane - step) % outer
            for i in range(2):
                full = lax.dynamic_update_slice(full, held[i][None, None], (where, i, 0, 0))
        return full.reshape(width, -1)

    def scatter_weights(partials):
        views = [p.reshape(outer, 2, block // 2, p.shape[1]) for p in partials]

        def own(step, i):
            where = (plane - 1 - step) % outer
            return jnp.concatenate(
                [
                    lax.dynamic_slice(v, (where, i, 0, 0), (1, 1) + v.shape[2:])[0, 0]
                    for v in views
                ],
                axis=1,
            )

        held = [own(0, 0), own(0, 1)]
        for step in range(1, outer):
            held = [hop(h) for h in held]
            held = [(held[i].astype(F32) + own(step, i).astype(F32)).astype(BF) for i in range(2)]
        pieces = exchange(jnp.concatenate(held, axis=0).reshape(INNER, part, -1))
        out, at = [], 0
        for p in partials:
            cut = slice(at, at + p.shape[1])
            out.append(jnp.concatenate([x[:, cut] for x in pieces], axis=1).astype(F32))
            at += p.shape[1]
        return out

    gains = jnp.stack([gain_self, gain_cross, gain_ffn]).astype(F32)
    away = swap(gains, 2)
    near = swap(jnp.stack([gains, away]), 1)
    held = jnp.concatenate(natural(gains, near[0], away, near[1]), axis=1)
    all_gains = jnp.zeros((outer, 3, block), F32)
    for step in range(outer):
        if step:
            held = small_hop(held)
        all_gains = lax.dynamic_update_slice(
            all_gains, held[None], ((plane - step) % outer, 0, 0)
        )
    gain_first, gain_second, gain_third = (all_gains[:, i].reshape(1, width) for i in range(3))

    row_count, length = segments.shape
    examples, patch_count, _ = patches.shape
    slot = jnp.take_along_axis(example_of, segments, axis=1)
    ids = rows_of(jnp.concatenate([segments, slot], axis=0))
    ids = ids.reshape(INNER, 2, row_count * length)
    seg_rows = ids[:, 0].reshape(INNER * row_count, length)
    slot_rows = ids[:, 1].reshape(INNER * row_count, length)
    key_slots = jnp.broadcast_to(
        (jnp.arange(examples * patch_count // row_count, dtype=jnp.int32) // patch_count),
        (INNER * row_count, 1, examples * patch_count // row_count),
    )
    self_ids = (seg_rows[:, :, None], seg_rows[:, None, :])
    cross_ids = (slot_rows[:, :, None], key_slots)

    w_self = gather_weights([wq_self, wk_self, wv_self, wo_self.T])
    w_cross = gather_weights([wq_cross, wk_cross, wv_cross, wo_cross.T])
    w_gu = gather_weights([w_gate, w_up])
    w_dn = gather_weights([w_down.T])
    hw = w_self.shape[1] // 4
    fw = w_dn.shape[1]

    start = inputs.astype(F32)
    normed, scale_self = rms(start, gain_first)
    normed_self = rows_of(normed)
    memory = rows_of(patches.reshape(-1, width))
    qkv = dot(normed_self, w_self[:, : 3 * hw], 1, 0).astype(BF)
    self_args = ((qkv, 0, hw), (qkv, 1, hw), (qkv, 2, hw))
    mixed_self = attend(True, *self_ids, *self_args)
    after_self = start + reduce_rows(dot(mixed_self, w_self[:, 3 * hw :], 1, 1))
    normed, scale_cross = rms(after_self, gain_second)
    normed_cross = rows_of(normed)
    kv = dot(memory, w_cross[:, hw : 3 * hw], 1, 0).astype(BF)
    q = dot(normed_cross, w_cross[:, :hw], 1, 0).astype(BF)
    cross_args = ((q, 0, hw), (kv, 0, hw), (kv, 1, hw))
    mixed_cross = attend(False, *cross_ids, *cross_args)
    after_cross = after_self + reduce_rows(dot(mixed_cross, w_cross[:, 3 * hw :], 1, 1))
    normed, scale_ffn = rms(after_cross, gain_third)
    normed_ffn = rows_of(normed)
    gu = dot(normed_ffn, w_gu, 1, 0)
    gate, up = gu[:, :fw], gu[:, fw:]
    value, slope = gelu_parts(gate)
    hidden = (value * up).astype(BF)
    output = after_cross + reduce_rows(dot(hidden, w_dn, 1, 1))

    grad_rows = rows_of(grad_out)
    term_down = dot(grad_rows, hidden, 0, 0).astype(BF)
    grad_hidden = dot(grad_rows, w_dn, 1, 0)
    grad_gu = jnp.concatenate(
        [(grad_hidden * up * slope).astype(BF), (grad_hidden * value).astype(BF)], axis=1
    )
    (grad_w_down,) = scatter_weights([term_down])
    term_gu = dot(normed_ffn, grad_gu, 0, 0).astype(BF)
    grad_w_gate, grad_w_up = scatter_weights([term_gu[:, :fw], term_gu[:, fw:]])
    grad, gain_grad_ffn = rms_back(
        after_cross, scale_ffn, gain_third, reduce_rows(dot(grad_gu, w_gu, 1, 1))
    )
    grad_after_cross = grad_out.astype(F32) + grad
    branch = rows_of(grad_after_cross.astype(BF))
    term_o = dot(branch, mixed_cross, 0, 0).astype(BF)
    grad_mixed = dot(branch, w_cross[:, 3 * hw :], 1, 0).astype(BF)
    grad_q, grad_kv = attend_back(False, *cross_ids, *cross_args, grad_mixed)
    term_q = dot(normed_cross, grad_q, 0, 0).astype(BF)
    term_kv = dot(memory, grad_kv, 0, 0).astype(BF)
    grad_normed = reduce_rows(dot(grad_q, w_cross[:, :hw], 1, 1))
    grad_wq_cross, grad_wk_cross, grad_wv_cross, grad_wo_cross = scatter_weights(
        [term_q, term_kv[:, :hw], term_kv[:, hw:], term_o]
    )
    grad_memory = reduce_rows(dot(grad_kv, w_cross[:, hw : 3 * hw], 1, 1))
    grad_patches = grad_memory.reshape(patches.shape)
    grad, gain_grad_cross = rms_back(after_self, scale_cross, gain_second, grad_normed)
    grad_after_self = grad_after_cross + grad
    branch = rows_of(grad_after_self.astype(BF))
    term_o = dot(branch, mixed_self, 0, 0).astype(BF)
    grad_mixed = dot(branch, w_self[:, 3 * hw :], 1, 0).astype(BF)
    grad_q, grad_kv = attend_back(True, *self_ids, *self_args, grad_mixed)
    grad_qkv = jnp.concatenate([grad_q, grad_kv], axis=1)
    term_qkv = dot(normed_self, grad_qkv, 0, 0).astype(BF)
    grad_wq_self, grad_wk_self, grad_wv_self, grad_wo_self = scatter_weights(
        [term_qkv[:, :hw], term_qkv[:, hw : 2 * hw], term_qkv[:, 2 * hw :], term_o]
    )
    grad_normed = reduce_rows(dot(grad_qkv, w_self[:, : 3 * hw], 1, 1))
    grad, gain_grad_self = rms_back(start, scale_self, gain_first, grad_normed)
    grad_inputs = grad_after_self + grad

    gain_grads = jnp.concatenate([gain_grad_self, gain_grad_cross, gain_grad_ffn], axis=0)
    gain_grads = gain_grads + swap(gain_grads, 2)
    gain_grads = gain_grads + swap(gain_grads, 1)

    def gain_block(step):
        return lax.dynamic_slice_in_dim(
            gain_grads, ((plane - 1 - step) % outer) * block, block, axis=1
        )

    held = gain_block(0)
    for step in range(1, outer):
        held = small_hop(held) + gain_block(step)
    held = lax.dynamic_slice_in_dim(held, mine * part, part, axis=1)

    return (
        output,
        grad_inputs,
        grad_patches,
        held[0],
        grad_wq_self,
        grad_wk_self,
        grad_wv_self,
        grad_wo_self.T,
        held[1],
        grad_wq_cross,
        grad_wk_cross,
        grad_wv_cross,
        grad_wo_cross.T,
        held[2],
        grad_w_gate,
        grad_w_up,
        grad_w_down.T,
    )


def solution(mesh):
    rows, cut, turned, gain = P("dp", None), P("dp", "mp"), P("mp", "dp"), P("dp")
    attention = (gain, cut, cut, cut, turned)
    weights = attention + attention + (gain, cut, cut, turned)
    return jax.shard_map(
        on_device,
        mesh=mesh,
        in_specs=(rows, rows, rows, P("dp", None, None), rows) + weights,
        out_specs=(rows, rows, P("dp", None, None)) + weights,
        check_vma=False,
    )
```

```python
import functools

import jax
import jax.numpy as jnp
from jax import lax
from jax.experimental import pallas as pl
from jax.experimental.pallas import tpu as pltpu
from jax.sharding import PartitionSpec as P

HEAD_DIM = 64
ATTN = 4
FFN = 4
EPS = 1e-06
NEG = -1e30
BF = jnp.bfloat16
F32 = jnp.float32


def dot(a, b, da, db):
    return lax.dot_general(a, b, (((da,), (db,)), ((), ())), preferred_element_type=F32)


def mask_of(qid_ref, kid_ref, causal):
    allowed = qid_ref[...] == kid_ref[...]
    if causal:
        rows = lax.broadcasted_iota(jnp.int32, allowed.shape, 0)
        cols = lax.broadcasted_iota(jnp.int32, allowed.shape, 1)
        allowed = allowed & (rows >= cols)
    return allowed


def soft(scores, allowed):
    scores = jnp.where(allowed, scores * HEAD_DIM ** (-0.5), NEG)
    raised = jnp.exp(scores - jnp.max(scores, axis=-1, keepdims=True))
    return raised * (1.0 / jnp.sum(raised, axis=-1, keepdims=True))


def heads_of(ref):
    return [ref[:, first : first + HEAD_DIM] for first in range(0, ref.shape[1], HEAD_DIM)]


def attend_kernel(causal, qid_ref, kid_ref, q_ref, k_ref, v_ref, out_ref):
    allowed = mask_of(qid_ref, kid_ref, causal)
    scores = jnp.stack([dot(q, k, 1, 1) for q, k in zip(heads_of(q_ref), heads_of(k_ref))])
    probs = soft(scores, allowed[None]).astype(BF)
    pieces = [dot(probs[h], v, 1, 0).astype(BF) for h, v in enumerate(heads_of(v_ref))]
    out_ref[...] = jnp.concatenate(pieces, axis=1)


def attend_back_kernel(causal, qid_ref, kid_ref, q_ref, k_ref, v_ref, g_ref, dq_ref, dkv_ref):
    allowed = mask_of(qid_ref, kid_ref, causal)
    scale = HEAD_DIM ** (-0.5)
    qs, ks, vs, gs = heads_of(q_ref), heads_of(k_ref), heads_of(v_ref), heads_of(g_ref)
    scores = jnp.stack([dot(q, k, 1, 1) for q, k in zip(qs, ks)])
    grad_probs = jnp.stack([dot(g, v, 1, 1) for g, v in zip(gs, vs)])
    probs = soft(scores, allowed[None])
    centre = jnp.sum(probs * grad_probs, axis=-1, keepdims=True)
    ds = (probs * (grad_probs - centre)).astype(BF)
    probs = probs.astype(BF)
    dvs = [dot(probs[h], g, 0, 0).astype(BF) for h, g in enumerate(gs)]
    dqs = [(dot(ds[h], k, 1, 0) * scale).astype(BF) for h, k in enumerate(ks)]
    dks = [(dot(ds[h], q, 0, 0) * scale).astype(BF) for h, q in enumerate(qs)]
    dq_ref[...] = jnp.concatenate(dqs, axis=1)
    dkv_ref[...] = jnp.concatenate(dks + dvs, axis=1)


def id_specs(length, keys):
    return [
        pl.BlockSpec((None, length, 1), lambda r: (r, 0, 0)),
        pl.BlockSpec((None, 1, keys), lambda r: (r, 0, 0)),
    ]


def attend(causal, qid, kid, q, k, v):
    rows, length, _ = qid.shape
    keys = kid.shape[2]
    width = q[2]
    specs = [
        pl.BlockSpec((n, width), functools.partial(lambda c, r: (r, c), col))
        for n, col in ((length, q[1]), (keys, k[1]), (keys, v[1]))
    ]
    return pl.pallas_call(
        functools.partial(attend_kernel, causal),
        grid=(rows,),
        in_specs=id_specs(length, keys) + specs,
        out_specs=pl.BlockSpec((length, width), lambda r: (r, 0)),
        out_shape=jax.ShapeDtypeStruct((rows * length, width), BF),
        cost_estimate=pl.CostEstimate(
            flops=4 * rows * length * keys * width,
            transcendentals=rows * length * keys * width // HEAD_DIM,
            bytes_accessed=8 * rows * length * width,
        ),
    )(qid, kid, q[0], k[0], v[0])


def attend_back(causal, qid, kid, q, k, v, g):
    rows, length, _ = qid.shape
    keys = kid.shape[2]
    width = q[2]
    specs = [
        pl.BlockSpec((n, width), functools.partial(lambda c, r: (r, c), col))
        for n, col in ((length, q[1]), (keys, k[1]), (keys, v[1]), (length, 0))
    ]
    return pl.pallas_call(
        functools.partial(attend_back_kernel, causal),
        grid=(rows,),
        in_specs=id_specs(length, keys) + specs,
        out_specs=[
            pl.BlockSpec((length, width), lambda r: (r, 0)),
            pl.BlockSpec((keys, 2 * width), lambda r: (r, 0)),
        ],
        out_shape=[
            jax.ShapeDtypeStruct((rows * length, width), BF),
            jax.ShapeDtypeStruct((rows * keys, 2 * width), BF),
        ],
        cost_estimate=pl.CostEstimate(
            flops=10 * rows * length * keys * width,
            transcendentals=rows * length * keys * width // HEAD_DIM,
            bytes_accessed=14 * rows * length * width,
        ),
    )(qid, kid, q[0], k[0], v[0], g)


def rms(values, gain):
    scale = lax.rsqrt(jnp.mean(values * values, axis=-1, keepdims=True) + EPS)
    return (values * scale * gain).astype(BF), scale


def rms_back(values, scale, gain, grad):
    weighted = grad * gain
    mean = jnp.mean(weighted * values, axis=-1, keepdims=True)
    return (
        scale * weighted - values * (scale * scale * scale) * mean,
        jnp.sum(grad * values * scale, axis=0, keepdims=True),
    )


def gelu_parts(gate):
    c = (2.0 / jnp.pi) ** 0.5
    inner = jnp.tanh(c * (gate + 0.044715 * gate * gate * gate))
    value = 0.5 * gate * (1.0 + inner)
    slope = 0.5 * (1.0 + inner) + 0.5 * gate * (1.0 - inner * inner) * c * (
        1.0 + 3 * 0.044715 * gate * gate
    )
    return value, slope


def on_device(
    inputs,
    segments,
    example_of,
    patches,
    grad_out,
    gain_self,
    wq_self,
    wk_self,
    wv_self,
    wo_self,
    gain_cross,
    wq_cross,
    wk_cross,
    wv_cross,
    wo_cross,
    gain_ffn,
    w_gate,
    w_up,
    w_down,
):
    dp = lax.axis_size("dp")
    place = lax.axis_index("dp")
    tokens, width = inputs.shape
    part = width // dp

    def tie(*values):
        return lax.optimization_barrier(values)

    def swap(value, distance):
        return lax.ppermute(value, "dp", [(i, i ^ distance) for i in range(dp)])

    def swap_mp(value):
        return lax.ppermute(value, "mp", [(0, 1), (1, 0)])

    def planes(inner):
        return [[m + inner * i for i in range(dp // inner)] for m in range(inner)]

    def rows_of(value, inner):
        even = [value] + [swap(value, d) for d in range(2, inner, 2)]
        odd = swap(jnp.stack(even), 1)
        return jnp.concatenate(
            [odd[d // 2] if d % 2 else even[d // 2] for d in range(inner)], axis=0
        )

    def reduce_rows(partial, inner):
        parts = partial.astype(BF).reshape(inner, -1, partial.shape[1])
        near = swap(jnp.stack([parts[d] for d in range(1, inner, 2)]), 1)
        total = parts[0].astype(F32) + near[0].astype(F32)
        for d in range(2, inner, 2):
            term = (parts[d].astype(F32) + near[d // 2].astype(F32)).astype(BF)
            total = total + swap(term, d).astype(F32)
        total = total.astype(BF)
        return total.astype(F32) + swap_mp(total).astype(F32)

    def exchange(blocks, inner):
        groups = [[m + inner * i for m in range(inner)] for i in range(dp // inner)]
        return lax.all_to_all(blocks, "dp", 0, 0, axis_index_groups=groups, tiled=True)

    def pack(weights, inner):
        return jnp.stack(
            [
                jnp.concatenate(
                    [
                        w[:, i * (w.shape[1] // inner) : (i + 1) * (w.shape[1] // inner)]
                        for w in weights
                    ],
                    axis=1,
                )
                for i in range(inner)
            ]
        )

    def over_planes(shard, inner):
        shard = shard.reshape(inner * part, -1)
        return lax.all_gather(shard, "dp", axis_index_groups=planes(inner), tiled=True)

    def scatter_weights(whole, widths, inner):
        held = lax.psum_scatter(whole, "dp", axis_index_groups=planes(inner), tiled=True)
        pieces = exchange(held.reshape(inner, part, -1), inner)
        out, at = [], 0
        for w in widths:
            cut = slice(at, at + w)
            out.append(jnp.concatenate([x[:, cut] for x in pieces], axis=1).astype(F32))
            at += w
        return out

    shard_self = exchange(pack([wq_self, wk_self, wv_self, wo_self.T], ATTN), ATTN)
    packed_cross = pack([wq_cross, wk_cross, wv_cross, wo_cross.T], ATTN)
    shard_self, inputs, packed_cross = tie(shard_self, inputs, packed_cross)
    w_self = over_planes(shard_self, ATTN)
    start_rows = rows_of(inputs, ATTN)
    shard_cross = exchange(packed_cross, ATTN)
    packed_ffn = pack([w_gate, w_up, w_down.T], FFN)
    shard_cross, patch_rows, packed_ffn = tie(shard_cross, patches.reshape(-1, width), packed_ffn)
    w_cross = over_planes(shard_cross, ATTN)
    memory = rows_of(patch_rows, ATTN)
    shard_ffn = exchange(packed_ffn, FFN)
    shard_ffn, grad_out = tie(shard_ffn, grad_out)
    grad_rows = rows_of(grad_out, FFN)
    start_rows, memory, grad_rows, shard_ffn = tie(start_rows, memory, grad_rows, shard_ffn)
    hw = w_self.shape[1] // 4

    gains = jnp.stack([gain_self, gain_cross, gain_ffn]).astype(F32)
    held = rows_of(jnp.stack([gains] + [swap(gains, d) for d in range(ATTN, dp, ATTN)])[None], ATTN)
    all_gains = jnp.zeros((dp, 3, part), F32)
    for i in range(dp // ATTN):
        for j in range(ATTN):
            all_gains = lax.dynamic_update_slice(
                all_gains, held[j, i][None], (place ^ (i * ATTN + j), 0, 0)
            )
    gain_first, gain_second, gain_third = (all_gains[:, i].reshape(1, width) for i in range(3))

    row_count, length = segments.shape
    examples, patch_count, _ = patches.shape
    slot = jnp.take_along_axis(example_of, segments, axis=1)
    ids = rows_of(jnp.concatenate([segments, slot], axis=0)[None], ATTN)
    seg_rows = ids[:, :row_count].reshape(ATTN * row_count, length)
    slot_rows = ids[:, row_count:].reshape(ATTN * row_count, length)
    key_slots = jnp.broadcast_to(
        (jnp.arange(examples * patch_count // row_count, dtype=jnp.int32) // patch_count),
        (ATTN * row_count, 1, examples * patch_count // row_count),
    )
    self_ids = (seg_rows[:, :, None], seg_rows[:, None, :])
    cross_ids = (slot_rows[:, :, None], key_slots)

    start = inputs.astype(F32)
    _, scale_self = rms(start, gain_first)
    normed_self, _ = rms(start_rows.astype(F32), gain_first)
    qkv = dot(normed_self, w_self[:, : 3 * hw], 1, 0).astype(BF)
    self_args = ((qkv, 0, hw), (qkv, 1, hw), (qkv, 2, hw))
    mixed_self = attend(True, *self_ids, *self_args)
    after_self = start + reduce_rows(dot(mixed_self, w_self[:, 3 * hw :], 1, 1), ATTN)
    normed, scale_cross = rms(after_self, gain_second)
    normed, shard_ffn = tie(normed, shard_ffn)
    normed_cross = rows_of(normed, ATTN)
    w_ffn = over_planes(shard_ffn, FFN)
    fw = w_ffn.shape[1] // 3
    w_gu, w_dn = w_ffn[:, : 2 * fw], w_ffn[:, 2 * fw :]
    kv = dot(memory, w_cross[:, hw : 3 * hw], 1, 0).astype(BF)
    q = dot(normed_cross, w_cross[:, :hw], 1, 0).astype(BF)
    cross_args = ((q, 0, hw), (kv, 0, hw), (kv, 1, hw))
    mixed_cross = attend(False, *cross_ids, *cross_args)
    after_cross = after_self + reduce_rows(dot(mixed_cross, w_cross[:, 3 * hw :], 1, 1), ATTN)
    normed, scale_ffn = rms(after_cross, gain_third)
    normed_ffn = rows_of(normed, FFN)
    gu = dot(normed_ffn, w_gu, 1, 0)
    gate, up = gu[:, :fw], gu[:, fw:]
    value, slope = gelu_parts(gate)
    hidden = (value * up).astype(BF)

    term_down = dot(grad_rows, hidden, 0, 0).astype(BF)
    grad_hidden = dot(grad_rows, w_dn, 1, 0)
    grad_gu = jnp.concatenate(
        [(grad_hidden * up * slope).astype(BF), (grad_hidden * value).astype(BF)], axis=1
    )
    term_gu = dot(normed_ffn, grad_gu, 0, 0).astype(BF)
    grad_gu, term_down, term_gu = tie(grad_gu, term_down, term_gu)
    (grad_w_down,) = scatter_weights(term_down, [fw], FFN)
    grad_w_gate, grad_w_up = scatter_weights(term_gu, [fw, fw], FFN)
    grad_normed = reduce_rows(dot(grad_gu, w_gu, 1, 1), FFN)
    grad, gain_grad_ffn = rms_back(after_cross, scale_ffn, gain_third, grad_normed)
    grad_after_cross = grad_out.astype(F32) + grad
    branch = rows_of(grad_after_cross.astype(BF), ATTN)
    branch, hidden = tie(branch, hidden)
    output = after_cross + reduce_rows(dot(hidden, w_dn, 1, 1), FFN)
    term_o = dot(branch, mixed_cross, 0, 0).astype(BF)
    grad_mixed = dot(branch, w_cross[:, 3 * hw :], 1, 0).astype(BF)
    grad_q, grad_kv = attend_back(False, *cross_ids, *cross_args, grad_mixed)
    term_q = dot(normed_cross, grad_q, 0, 0).astype(BF)
    term_kv = dot(memory, grad_kv, 0, 0).astype(BF)
    grad_normed = reduce_rows(dot(grad_q, w_cross[:, :hw], 1, 1), ATTN)
    grad_wq_cross, grad_wk_cross, grad_wv_cross, grad_wo_cross = scatter_weights(
        jnp.concatenate([term_q, term_kv, term_o], axis=1), [hw] * 4, ATTN
    )
    grad, gain_grad_cross = rms_back(after_self, scale_cross, gain_second, grad_normed)
    grad_after_self = grad_after_cross + grad
    branch = rows_of(grad_after_self.astype(BF), ATTN)
    branch, grad_kv = tie(branch, grad_kv)
    grad_memory = reduce_rows(dot(grad_kv, w_cross[:, hw : 3 * hw], 1, 1), ATTN)
    grad_patches = grad_memory.reshape(patches.shape)
    term_o = dot(branch, mixed_self, 0, 0).astype(BF)
    grad_mixed = dot(branch, w_self[:, 3 * hw :], 1, 0).astype(BF)
    grad_q, grad_kv = attend_back(True, *self_ids, *self_args, grad_mixed)
    grad_qkv = jnp.concatenate([grad_q, grad_kv], axis=1)
    term_qkv = dot(normed_self, grad_qkv, 0, 0).astype(BF)
    term_self = jnp.concatenate([term_qkv, term_o], axis=1)
    grad_qkv, term_self = tie(grad_qkv, term_self)
    grad_wq_self, grad_wk_self, grad_wv_self, grad_wo_self = scatter_weights(
        term_self, [hw] * 4, ATTN
    )
    grad_normed = reduce_rows(dot(grad_qkv, w_self[:, : 3 * hw], 1, 1), ATTN)
    grad, gain_grad_self = rms_back(start, scale_self, gain_first, grad_normed)
    grad_inputs = grad_after_self + grad

    gain_grads = jnp.concatenate([gain_grad_self, gain_grad_cross, gain_grad_ffn], axis=0)
    gain_grads, grad_w_down, grad_wo_cross = tie(gain_grads, grad_w_down, grad_wo_cross)
    bit = 1
    while bit < dp:
        gain_grads = gain_grads + swap(gain_grads, bit)
        bit *= 2
    held = lax.dynamic_slice_in_dim(gain_grads, place * part, part, axis=1)

    return (
        output,
        grad_inputs,
        grad_patches,
        held[0],
        grad_wq_self,
        grad_wk_self,
        grad_wv_self,
        grad_wo_self.T,
        held[1],
        grad_wq_cross,
        grad_wk_cross,
        grad_wv_cross,
        grad_wo_cross.T,
        held[2],
        grad_w_gate,
        grad_w_up,
        grad_w_down.T,
    )


def solution(mesh):
    rows, cut, turned, gain = P("dp", None), P("dp", "mp"), P("mp", "dp"), P("dp")
    attention = (gain, cut, cut, cut, turned)
    weights = attention + attention + (gain, cut, cut, turned)
    return jax.shard_map(
        on_device,
        mesh=mesh,
        in_specs=(rows, rows, rows, P("dp", None, None), rows) + weights,
        out_specs=(rows, rows, P("dp", None, None)) + weights,
        check_vma=False,
    )
```

```python
import functools

import jax
import jax.numpy as jnp
from jax import lax
from jax.experimental.layout import Layout, with_layout_constraint
from jax.experimental import pallas as pl
from jax.experimental.pallas import tpu as pltpu
from jax.sharding import PartitionSpec as P

HEAD_DIM = 64
ATTN = 4
FFN = 4
EPS = 1e-06
NEG = -1e30
BF = jnp.bfloat16
F32 = jnp.float32


def dot(a, b, da, db):
    return lax.dot_general(a, b, (((da,), (db,)), ((), ())), preferred_element_type=F32)


def mask_of(qid_ref, kid_ref, causal):
    allowed = qid_ref[...] == kid_ref[...]
    if causal:
        rows = lax.broadcasted_iota(jnp.int32, allowed.shape, 0)
        cols = lax.broadcasted_iota(jnp.int32, allowed.shape, 1)
        allowed = allowed & (rows >= cols)
    return allowed


def soft(scores, allowed):
    scores = jnp.where(allowed, scores * HEAD_DIM ** (-0.5), NEG)
    raised = jnp.exp(scores - jnp.max(scores, axis=-1, keepdims=True))
    return raised * (1.0 / jnp.sum(raised, axis=-1, keepdims=True))


def heads_of(ref):
    return [ref[:, first : first + HEAD_DIM] for first in range(0, ref.shape[1], HEAD_DIM)]


def attend_kernel(causal, qid_ref, kid_ref, q_ref, k_ref, v_ref, out_ref):
    allowed = mask_of(qid_ref, kid_ref, causal)
    scores = jnp.stack([dot(q, k, 1, 1) for q, k in zip(heads_of(q_ref), heads_of(k_ref))])
    probs = soft(scores, allowed[None]).astype(BF)
    pieces = [dot(probs[h], v, 1, 0).astype(BF) for h, v in enumerate(heads_of(v_ref))]
    out_ref[...] = jnp.concatenate(pieces, axis=1)


def attend_back_kernel(causal, qid_ref, kid_ref, q_ref, k_ref, v_ref, g_ref, dq_ref, dkv_ref):
    allowed = mask_of(qid_ref, kid_ref, causal)
    scale = HEAD_DIM ** (-0.5)
    qs, ks, vs, gs = heads_of(q_ref), heads_of(k_ref), heads_of(v_ref), heads_of(g_ref)
    scores = jnp.stack([dot(q, k, 1, 1) for q, k in zip(qs, ks)])
    grad_probs = jnp.stack([dot(g, v, 1, 1) for g, v in zip(gs, vs)])
    probs = soft(scores, allowed[None])
    centre = jnp.sum(probs * grad_probs, axis=-1, keepdims=True)
    ds = (probs * (grad_probs - centre)).astype(BF)
    probs = probs.astype(BF)
    dvs = [dot(probs[h], g, 0, 0).astype(BF) for h, g in enumerate(gs)]
    dqs = [(dot(ds[h], k, 1, 0) * scale).astype(BF) for h, k in enumerate(ks)]
    dks = [(dot(ds[h], q, 0, 0) * scale).astype(BF) for h, q in enumerate(qs)]
    dq_ref[...] = jnp.concatenate(dqs, axis=1)
    dkv_ref[...] = jnp.concatenate(dks + dvs, axis=1)


def id_specs(length, keys):
    return [
        pl.BlockSpec((None, length, 1), lambda r: (r, 0, 0)),
        pl.BlockSpec((None, 1, keys), lambda r: (r, 0, 0)),
    ]


def attend(causal, qid, kid, q, k, v):
    rows, length, _ = qid.shape
    keys = kid.shape[2]
    width = q[2]
    specs = [
        pl.BlockSpec((n, width), functools.partial(lambda c, r: (r, c), col))
        for n, col in ((length, q[1]), (keys, k[1]), (keys, v[1]))
    ]
    return pl.pallas_call(
        functools.partial(attend_kernel, causal),
        grid=(rows,),
        in_specs=id_specs(length, keys) + specs,
        out_specs=pl.BlockSpec((length, width), lambda r: (r, 0)),
        out_shape=jax.ShapeDtypeStruct((rows * length, width), BF),
        cost_estimate=pl.CostEstimate(
            flops=4 * rows * length * keys * width,
            transcendentals=rows * length * keys * width // HEAD_DIM,
            bytes_accessed=8 * rows * length * width,
        ),
    )(qid, kid, q[0], k[0], v[0])


def attend_back(causal, qid, kid, q, k, v, g):
    rows, length, _ = qid.shape
    keys = kid.shape[2]
    width = q[2]
    specs = [
        pl.BlockSpec((n, width), functools.partial(lambda c, r: (r, c), col))
        for n, col in ((length, q[1]), (keys, k[1]), (keys, v[1]), (length, 0))
    ]
    return pl.pallas_call(
        functools.partial(attend_back_kernel, causal),
        grid=(rows,),
        in_specs=id_specs(length, keys) + specs,
        out_specs=[
            pl.BlockSpec((length, width), lambda r: (r, 0)),
            pl.BlockSpec((keys, 2 * width), lambda r: (r, 0)),
        ],
        out_shape=[
            jax.ShapeDtypeStruct((rows * length, width), BF),
            jax.ShapeDtypeStruct((rows * keys, 2 * width), BF),
        ],
        cost_estimate=pl.CostEstimate(
            flops=10 * rows * length * keys * width,
            transcendentals=rows * length * keys * width // HEAD_DIM,
            bytes_accessed=14 * rows * length * width,
        ),
    )(qid, kid, q[0], k[0], v[0], g)


def term(source, grad):
    return with_layout_constraint(dot(source, grad, 0, 0).astype(BF), Layout((0, 1)))


def rms(values, gain):
    scale = lax.rsqrt(jnp.mean(values * values, axis=-1, keepdims=True) + EPS)
    return (values * scale * gain).astype(BF), scale


def rms_back(values, scale, gain, grad):
    weighted = grad * gain
    mean = jnp.mean(weighted * values, axis=-1, keepdims=True)
    return (
        scale * weighted - values * (scale * scale * scale) * mean,
        jnp.sum(grad * values * scale, axis=0, keepdims=True),
    )


def gelu_parts(gate):
    c = (2.0 / jnp.pi) ** 0.5
    inner = jnp.tanh(c * (gate + 0.044715 * gate * gate * gate))
    value = 0.5 * gate * (1.0 + inner)
    slope = 0.5 * (1.0 + inner) + 0.5 * gate * (1.0 - inner * inner) * c * (
        1.0 + 3 * 0.044715 * gate * gate
    )
    return value, slope


def on_device(
    inputs,
    segments,
    example_of,
    patches,
    grad_out,
    gain_self,
    wq_self,
    wk_self,
    wv_self,
    wo_self,
    gain_cross,
    wq_cross,
    wk_cross,
    wv_cross,
    wo_cross,
    gain_ffn,
    w_gate,
    w_up,
    w_down,
):
    dp = lax.axis_size("dp")
    place = lax.axis_index("dp")
    tokens, width = inputs.shape
    part = width // dp

    def tie(*values):
        return lax.optimization_barrier(values)

    def swap(value, distance):
        return lax.ppermute(value, "dp", [(i, i ^ distance) for i in range(dp)])

    def swap_mp(value):
        return lax.ppermute(value, "mp", [(0, 1), (1, 0)])

    def planes(inner):
        return [[m + inner * i for i in range(dp // inner)] for m in range(inner)]

    def rows_of(value, inner):
        even = [value] + [swap(value, d) for d in range(2, inner, 2)]
        odd = swap(jnp.stack(even), 1)
        return jnp.concatenate(
            [odd[d // 2] if d % 2 else even[d // 2] for d in range(inner)], axis=0
        )

    def reduce_rows(partial, inner):
        parts = partial.astype(BF).reshape(inner, -1, partial.shape[1])
        near = swap(jnp.stack([parts[d] for d in range(1, inner, 2)]), 1)
        total = parts[0].astype(F32) + near[0].astype(F32)
        for d in range(2, inner, 2):
            term = (parts[d].astype(F32) + near[d // 2].astype(F32)).astype(BF)
            total = total + swap(term, d).astype(F32)
        total = total.astype(BF)
        return total.astype(F32) + swap_mp(total).astype(F32)

    def exchange(blocks, inner):
        groups = [[m + inner * i for m in range(inner)] for i in range(dp // inner)]
        return lax.all_to_all(blocks, "dp", 0, 0, axis_index_groups=groups, tiled=True)

    def pack(weights, inner):
        return jnp.stack(
            [
                jnp.concatenate(
                    [
                        w[:, i * (w.shape[1] // inner) : (i + 1) * (w.shape[1] // inner)]
                        for w in weights
                    ],
                    axis=1,
                )
                for i in range(inner)
            ]
        )

    def over_planes(shard, inner):
        shard = shard.reshape(inner * part, -1)
        return lax.all_gather(shard, "dp", axis_index_groups=planes(inner), tiled=True)

    def plane_sum(whole, inner):
        return lax.psum_scatter(whole, "dp", axis_index_groups=planes(inner), tiled=True)

    def split(pieces, widths):
        out, at = [], 0
        for w in widths:
            cut = slice(at, at + w)
            out.append(jnp.concatenate([x[:, cut] for x in pieces], axis=1).astype(F32))
            at += w
        return out

    def scatter_weights(whole, widths, inner):
        held = plane_sum(whole, inner).reshape(inner, part, -1)
        return split(exchange(held, inner), widths)

    packed_self = pack([wq_self, wk_self, wv_self, wo_self.T], ATTN)
    shard_self = exchange(packed_self, ATTN)
    packed_cross = pack([wq_cross, wk_cross, wv_cross, wo_cross.T], ATTN)
    shard_self, inputs, packed_cross, gain_self, segments = tie(
        shard_self, inputs, packed_cross, gain_self, segments
    )
    w_self = over_planes(shard_self, ATTN)
    start_rows = rows_of(inputs, ATTN)
    shard_cross = exchange(packed_cross, ATTN)
    packed_ffn = pack([w_gate, w_up, w_down.T], FFN)
    shard_cross, patch_rows, packed_ffn = tie(shard_cross, patches.reshape(-1, width), packed_ffn)
    w_cross = over_planes(shard_cross, ATTN)
    memory = rows_of(patch_rows, ATTN)
    shard_ffn = exchange(packed_ffn, FFN)
    shard_ffn, grad_out = tie(shard_ffn, grad_out)
    grad_rows = rows_of(grad_out, FFN)
    start_rows, memory, grad_rows, shard_ffn = tie(start_rows, memory, grad_rows, shard_ffn)
    hw = w_self.shape[1] // 4

    gains = jnp.stack([gain_self, gain_cross, gain_ffn]).astype(F32)
    held = rows_of(jnp.stack([gains] + [swap(gains, d) for d in range(ATTN, dp, ATTN)])[None], ATTN)
    all_gains = jnp.zeros((dp, 3, part), F32)
    for i in range(dp // ATTN):
        for j in range(ATTN):
            all_gains = lax.dynamic_update_slice(
                all_gains, held[j, i][None], (place ^ (i * ATTN + j), 0, 0)
            )
    gain_first, gain_second, gain_third = (all_gains[:, i].reshape(1, width) for i in range(3))

    row_count, length = segments.shape
    examples, patch_count, _ = patches.shape
    slot = jnp.take_along_axis(example_of, segments, axis=1)
    ids = rows_of(jnp.concatenate([segments, slot], axis=0)[None], ATTN)
    seg_rows = ids[:, :row_count].reshape(ATTN * row_count, length)
    slot_rows = ids[:, row_count:].reshape(ATTN * row_count, length)
    key_slots = jnp.broadcast_to(
        (jnp.arange(examples * patch_count // row_count, dtype=jnp.int32) // patch_count),
        (ATTN * row_count, 1, examples * patch_count // row_count),
    )
    self_ids = (seg_rows[:, :, None], seg_rows[:, None, :])
    cross_ids = (slot_rows[:, :, None], key_slots)

    start = inputs.astype(F32)
    _, scale_self = rms(start, gain_first)
    normed_self, _ = rms(start_rows.astype(F32), gain_first)
    qkv = dot(normed_self, w_self[:, : 3 * hw], 1, 0).astype(BF)
    self_args = ((qkv, 0, hw), (qkv, 1, hw), (qkv, 2, hw))
    mixed_self = attend(True, *self_ids, *self_args)
    after_self = start + reduce_rows(dot(mixed_self, w_self[:, 3 * hw :], 1, 1), ATTN)
    normed, scale_cross = rms(after_self, gain_second)
    normed, shard_ffn = tie(normed, shard_ffn)
    normed_cross = rows_of(normed, ATTN)
    w_ffn = over_planes(shard_ffn, FFN)
    fw = w_ffn.shape[1] // 3
    w_gu, w_dn = w_ffn[:, : 2 * fw], w_ffn[:, 2 * fw :]
    kv = dot(memory, w_cross[:, hw : 3 * hw], 1, 0).astype(BF)
    q = dot(normed_cross, w_cross[:, :hw], 1, 0).astype(BF)
    cross_args = ((q, 0, hw), (kv, 0, hw), (kv, 1, hw))
    mixed_cross = attend(False, *cross_ids, *cross_args)
    after_cross = after_self + reduce_rows(dot(mixed_cross, w_cross[:, 3 * hw :], 1, 1), ATTN)
    normed, scale_ffn = rms(after_cross, gain_third)
    normed_ffn = rows_of(normed, FFN)
    gu = dot(normed_ffn, w_gu, 1, 0)
    gate, up = gu[:, :fw], gu[:, fw:]
    value, slope = gelu_parts(gate)
    hidden = (value * up).astype(BF)

    term_down = term(grad_rows, hidden)
    grad_hidden = dot(grad_rows, w_dn, 1, 0)
    grad_gu = jnp.concatenate(
        [(grad_hidden * up * slope).astype(BF), (grad_hidden * value).astype(BF)], axis=1
    )
    term_gu = term(normed_ffn, grad_gu)
    grad_gu, term_down, term_gu = tie(grad_gu, term_down, term_gu)
    (grad_w_down,) = scatter_weights(term_down, [fw], FFN)
    grad_w_gate, grad_w_up = scatter_weights(term_gu, [fw, fw], FFN)
    grad_normed = reduce_rows(dot(grad_gu, w_gu, 1, 1), FFN)
    grad, gain_grad_ffn = rms_back(after_cross, scale_ffn, gain_third, grad_normed)
    grad_after_cross = grad_out.astype(F32) + grad
    branch = rows_of(grad_after_cross.astype(BF), ATTN)
    branch, hidden = tie(branch, hidden)
    output = after_cross + reduce_rows(dot(hidden, w_dn, 1, 1), FFN)
    term_o = term(branch, mixed_cross)
    grad_mixed = dot(branch, w_cross[:, 3 * hw :], 1, 0).astype(BF)
    grad_q, grad_kv = attend_back(False, *cross_ids, *cross_args, grad_mixed)
    term_q = term(normed_cross, grad_q)
    term_kv = term(memory, grad_kv)
    grad_normed = reduce_rows(dot(grad_q, w_cross[:, :hw], 1, 1), ATTN)
    grad_wq_cross, grad_wk_cross, grad_wv_cross, grad_wo_cross = scatter_weights(
        jnp.concatenate([term_q, term_kv, term_o], axis=1), [hw] * 4, ATTN
    )
    grad, gain_grad_cross = rms_back(after_self, scale_cross, gain_second, grad_normed)
    grad_after_self = grad_after_cross + grad
    branch = rows_of(grad_after_self.astype(BF), ATTN)
    branch, grad_kv = tie(branch, grad_kv)
    grad_memory = reduce_rows(dot(grad_kv, w_cross[:, hw : 3 * hw], 1, 1), ATTN)
    grad_patches = grad_memory.reshape(patches.shape)
    term_o = term(branch, mixed_self)
    grad_mixed = dot(branch, w_self[:, 3 * hw :], 1, 0).astype(BF)
    grad_q, grad_kv = attend_back(True, *self_ids, *self_args, grad_mixed)
    grad_qkv = jnp.concatenate([grad_q, grad_kv], axis=1)
    term_qkv = term(normed_self, grad_qkv)
    term_self = jnp.concatenate([term_qkv, term_o], axis=1)
    grad_qkv, term_self = tie(grad_qkv, term_self)
    term_self = lax.all_to_all(
        term_self.reshape(-1, ATTN, part, 4 * hw),
        "dp",
        1,
        1,
        axis_index_groups=[[m + ATTN * i for m in range(ATTN)] for i in range(dp // ATTN)],
        tiled=True,
    )
    term_self = plane_sum(term_self.reshape(width, -1), ATTN).reshape(ATTN, part, -1)
    grad_wq_self, grad_wk_self, grad_wv_self, grad_wo_self = split(term_self, [hw] * 4)
    grad_normed = reduce_rows(dot(grad_qkv, w_self[:, : 3 * hw], 1, 1), ATTN)
    grad, gain_grad_self = rms_back(start, scale_self, gain_first, grad_normed)
    grad_inputs = grad_after_self + grad

    gain_grads = jnp.concatenate([gain_grad_self, gain_grad_cross, gain_grad_ffn], axis=0)
    bit = 1
    while bit < dp:
        gain_grads = gain_grads + swap(gain_grads, bit)
        bit *= 2
    held = lax.dynamic_slice_in_dim(gain_grads, place * part, part, axis=1)

    return (
        output,
        grad_inputs,
        grad_patches,
        held[0],
        grad_wq_self,
        grad_wk_self,
        grad_wv_self,
        grad_wo_self.T,
        held[1],
        grad_wq_cross,
        grad_wk_cross,
        grad_wv_cross,
        grad_wo_cross.T,
        held[2],
        grad_w_gate,
        grad_w_up,
        grad_w_down.T,
    )


def solution(mesh):
    rows, cut, turned, gain = P("dp", None), P("dp", "mp"), P("mp", "dp"), P("dp")
    attention = (gain, cut, cut, cut, turned)
    weights = attention + attention + (gain, cut, cut, turned)
    return jax.shard_map(
        on_device,
        mesh=mesh,
        in_specs=(rows, rows, rows, P("dp", None, None), rows) + weights,
        out_specs=(rows, rows, P("dp", None, None)) + weights,
        check_vma=False,
    )
```

```python
import functools

import jax
import jax.numpy as jnp
from jax import lax
from jax.experimental.layout import Layout, with_layout_constraint
from jax.experimental import pallas as pl
from jax.experimental.pallas import tpu as pltpu
from jax.sharding import PartitionSpec as P

HEAD_DIM = 64
ATTN = 4
FFN = 4
EPS = 1e-06
NEG = -1e30
BF = jnp.bfloat16
F32 = jnp.float32


def dot(a, b, da, db):
    return lax.dot_general(a, b, (((da,), (db,)), ((), ())), preferred_element_type=F32)


def mask_of(qid_ref, kid_ref, causal):
    allowed = qid_ref[...] == kid_ref[...]
    if causal:
        rows = lax.broadcasted_iota(jnp.int32, allowed.shape, 0)
        cols = lax.broadcasted_iota(jnp.int32, allowed.shape, 1)
        allowed = allowed & (rows >= cols)
    return allowed


def soft(scores, allowed):
    scores = jnp.where(allowed, scores * HEAD_DIM ** (-0.5), NEG)
    raised = jnp.exp(scores - jnp.max(scores, axis=-1, keepdims=True))
    return raised * (1.0 / jnp.sum(raised, axis=-1, keepdims=True))


def heads_of(ref):
    return [ref[:, first : first + HEAD_DIM] for first in range(0, ref.shape[1], HEAD_DIM)]


def attend_kernel(causal, qid_ref, kid_ref, q_ref, k_ref, v_ref, out_ref):
    allowed = mask_of(qid_ref, kid_ref, causal)
    scores = jnp.stack([dot(q, k, 1, 1) for q, k in zip(heads_of(q_ref), heads_of(k_ref))])
    probs = soft(scores, allowed[None]).astype(BF)
    pieces = [dot(probs[h], v, 1, 0).astype(BF) for h, v in enumerate(heads_of(v_ref))]
    out_ref[...] = jnp.concatenate(pieces, axis=1)


def attend_back_kernel(causal, qid_ref, kid_ref, q_ref, k_ref, v_ref, g_ref, dq_ref, dkv_ref):
    allowed = mask_of(qid_ref, kid_ref, causal)
    scale = HEAD_DIM ** (-0.5)
    qs, ks, vs, gs = heads_of(q_ref), heads_of(k_ref), heads_of(v_ref), heads_of(g_ref)
    scores = jnp.stack([dot(q, k, 1, 1) for q, k in zip(qs, ks)])
    grad_probs = jnp.stack([dot(g, v, 1, 1) for g, v in zip(gs, vs)])
    probs = soft(scores, allowed[None])
    centre = jnp.sum(probs * grad_probs, axis=-1, keepdims=True)
    ds = (probs * (grad_probs - centre)).astype(BF)
    probs = probs.astype(BF)
    dvs = [dot(probs[h], g, 0, 0).astype(BF) for h, g in enumerate(gs)]
    dqs = [(dot(ds[h], k, 1, 0) * scale).astype(BF) for h, k in enumerate(ks)]
    dks = [(dot(ds[h], q, 0, 0) * scale).astype(BF) for h, q in enumerate(qs)]
    dq_ref[...] = jnp.concatenate(dqs, axis=1)
    dkv_ref[...] = jnp.concatenate(dks + dvs, axis=1)


def id_specs(length, keys):
    return [
        pl.BlockSpec((None, length, 1), lambda r: (r, 0, 0)),
        pl.BlockSpec((None, 1, keys), lambda r: (r, 0, 0)),
    ]


def attend(causal, qid, kid, q, k, v):
    rows, length, _ = qid.shape
    keys = kid.shape[2]
    width = q[2]
    specs = [
        pl.BlockSpec((n, width), functools.partial(lambda c, r: (r, c), col))
        for n, col in ((length, q[1]), (keys, k[1]), (keys, v[1]))
    ]
    return pl.pallas_call(
        functools.partial(attend_kernel, causal),
        grid=(rows,),
        in_specs=id_specs(length, keys) + specs,
        out_specs=pl.BlockSpec((length, width), lambda r: (r, 0)),
        out_shape=jax.ShapeDtypeStruct((rows * length, width), BF),
        cost_estimate=pl.CostEstimate(
            flops=4 * rows * length * keys * width,
            transcendentals=rows * length * keys * width // HEAD_DIM,
            bytes_accessed=8 * rows * length * width,
        ),
    )(qid, kid, q[0], k[0], v[0])


def attend_back(causal, qid, kid, q, k, v, g):
    rows, length, _ = qid.shape
    keys = kid.shape[2]
    width = q[2]
    specs = [
        pl.BlockSpec((n, width), functools.partial(lambda c, r: (r, c), col))
        for n, col in ((length, q[1]), (keys, k[1]), (keys, v[1]), (length, 0))
    ]
    return pl.pallas_call(
        functools.partial(attend_back_kernel, causal),
        grid=(rows,),
        in_specs=id_specs(length, keys) + specs,
        out_specs=[
            pl.BlockSpec((length, width), lambda r: (r, 0)),
            pl.BlockSpec((keys, 2 * width), lambda r: (r, 0)),
        ],
        out_shape=[
            jax.ShapeDtypeStruct((rows * length, width), BF),
            jax.ShapeDtypeStruct((rows * keys, 2 * width), BF),
        ],
        cost_estimate=pl.CostEstimate(
            flops=10 * rows * length * keys * width,
            transcendentals=rows * length * keys * width // HEAD_DIM,
            bytes_accessed=14 * rows * length * width,
        ),
    )(qid, kid, q[0], k[0], v[0], g)


def term(source, grad):
    return with_layout_constraint(dot(source, grad, 0, 0).astype(BF), Layout((0, 1)))


def rms(values, gain):
    scale = lax.rsqrt(jnp.mean(values * values, axis=-1, keepdims=True) + EPS)
    return (values * scale * gain).astype(BF), scale


def rms_back(values, scale, gain, grad):
    weighted = grad * gain
    mean = jnp.mean(weighted * values, axis=-1, keepdims=True)
    return (
        scale * weighted - values * (scale * scale * scale) * mean,
        jnp.sum(grad * values * scale, axis=0, keepdims=True),
    )


def gelu_parts(gate):
    c = (2.0 / jnp.pi) ** 0.5
    inner = jnp.tanh(c * (gate + 0.044715 * gate * gate * gate))
    value = 0.5 * gate * (1.0 + inner)
    slope = 0.5 * (1.0 + inner) + 0.5 * gate * (1.0 - inner * inner) * c * (
        1.0 + 3 * 0.044715 * gate * gate
    )
    return value, slope


def on_device(
    inputs,
    segments,
    example_of,
    patches,
    grad_out,
    gain_self,
    wq_self,
    wk_self,
    wv_self,
    wo_self,
    gain_cross,
    wq_cross,
    wk_cross,
    wv_cross,
    wo_cross,
    gain_ffn,
    w_gate,
    w_up,
    w_down,
):
    dp = lax.axis_size("dp")
    place = lax.axis_index("dp")
    tokens, width = inputs.shape
    part = width // dp

    def tie(*values):
        return lax.optimization_barrier(values)

    def swap(value, distance):
        return lax.ppermute(value, "dp", [(i, i ^ distance) for i in range(dp)])

    def swap_mp(value):
        return lax.ppermute(value, "mp", [(0, 1), (1, 0)])

    def planes(inner):
        return [[m + inner * i for i in range(dp // inner)] for m in range(inner)]

    def rows_of(value, inner):
        even = [value] + [swap(value, d) for d in range(2, inner, 2)]
        odd = swap(jnp.stack(even), 1)
        return jnp.concatenate(
            [odd[d // 2] if d % 2 else even[d // 2] for d in range(inner)], axis=0
        )

    def reduce_rows(partial, inner):
        parts = partial.astype(BF).reshape(inner, -1, partial.shape[1])
        near = swap(jnp.stack([parts[d] for d in range(1, inner, 2)]), 1)
        total = parts[0].astype(F32) + near[0].astype(F32)
        for d in range(2, inner, 2):
            term = (parts[d].astype(F32) + near[d // 2].astype(F32)).astype(BF)
            total = total + swap(term, d).astype(F32)
        total = total.astype(BF)
        return total.astype(F32) + swap_mp(total).astype(F32)

    def exchange(blocks, inner):
        groups = [[m + inner * i for m in range(inner)] for i in range(dp // inner)]
        return lax.all_to_all(blocks, "dp", 0, 0, axis_index_groups=groups, tiled=True)

    def pack(weights, inner):
        return jnp.stack(
            [
                jnp.concatenate(
                    [
                        w[:, i * (w.shape[1] // inner) : (i + 1) * (w.shape[1] // inner)]
                        for w in weights
                    ],
                    axis=1,
                )
                for i in range(inner)
            ]
        )

    def over_planes(shard, inner):
        shard = shard.reshape(inner * part, -1)
        return lax.all_gather(shard, "dp", axis_index_groups=planes(inner), tiled=True)

    def ring_start(own, shard):
        block = [
            lax.dynamic_index_in_dim(shard, (place % ATTN) ^ j, 0, keepdims=False)
            for j in range(1, ATTN)
        ]
        return [own[None], block[0][None], jnp.stack(block[1:])]

    def ring_step(held):
        return [lax.ppermute(h, "dp", [(i, (i + ATTN) % dp) for i in range(dp)]) for h in held]

    def placed(kept):
        mine, plane, outer = place % ATTN, place // ATTN, dp // ATTN
        full = jnp.zeros((width, kept[0][0].shape[2]), BF)
        for step, held in enumerate(kept):
            for h, js in zip(held, ((0,), (1,), (2, 3))):
                for n, j in enumerate(js):
                    at = (((plane - step) % outer) * ATTN + (mine ^ j)) * part
                    full = lax.dynamic_update_slice(full, h[n], (at, 0))
        return full

    def plane_sum(whole, inner):
        return lax.psum_scatter(whole, "dp", axis_index_groups=planes(inner), tiled=True)

    def split(pieces, widths):
        out, at = [], 0
        for w in widths:
            cut = slice(at, at + w)
            out.append(jnp.concatenate([x[:, cut] for x in pieces], axis=1).astype(F32))
            at += w
        return out

    def scatter_weights(whole, widths, inner):
        held = plane_sum(whole, inner).reshape(inner, part, -1)
        return split(exchange(held, inner), widths)

    packed_self = pack([wq_self, wk_self, wv_self, wo_self.T], ATTN)
    own_self = lax.dynamic_index_in_dim(packed_self, place % ATTN, 0, keepdims=False)
    shard_self = exchange(packed_self, ATTN)
    packed_cross = pack([wq_cross, wk_cross, wv_cross, wo_cross.T], ATTN)
    ring = dp // ATTN == 4
    if ring:
        kept = [ring_start(own_self, shard_self)]
        kept.append(ring_step(kept[0]))
        kept[1][2], inputs, packed_cross = tie(kept[1][2], inputs, packed_cross)
        kept.append(ring_step(kept[1]))
        kept[2][2], gain_self, segments = tie(kept[2][2], gain_self, segments)
        kept.append(ring_step(kept[2]))
    else:
        shard_self, inputs, packed_cross = tie(shard_self, inputs, packed_cross)
        w_self = over_planes(shard_self, ATTN)
    start_rows = rows_of(inputs, ATTN)
    shard_cross = exchange(packed_cross, ATTN)
    packed_ffn = pack([w_gate, w_up, w_down.T], FFN)
    patch_rows = patches.reshape(-1, width)
    if ring:
        kept[3][2], shard_cross, start_rows, patch_rows, packed_ffn, grad_out = tie(
            kept[3][2], shard_cross, start_rows, patch_rows, packed_ffn, grad_out
        )
        w_self = placed(kept)
    w_cross = over_planes(shard_cross, ATTN)
    memory = rows_of(patch_rows, ATTN)
    shard_ffn = exchange(packed_ffn, FFN)
    shard_ffn, grad_out, memory = tie(shard_ffn, grad_out, memory)
    grad_rows = rows_of(grad_out, FFN)
    hw = w_self.shape[1] // 4

    gains = jnp.stack([gain_self, gain_cross, gain_ffn]).astype(F32)
    held = rows_of(jnp.stack([gains] + [swap(gains, d) for d in range(ATTN, dp, ATTN)])[None], ATTN)
    all_gains = jnp.zeros((dp, 3, part), F32)
    for i in range(dp // ATTN):
        for j in range(ATTN):
            all_gains = lax.dynamic_update_slice(
                all_gains, held[j, i][None], (place ^ (i * ATTN + j), 0, 0)
            )
    gain_first, gain_second, gain_third = (all_gains[:, i].reshape(1, width) for i in range(3))

    row_count, length = segments.shape
    examples, patch_count, _ = patches.shape
    slot = jnp.take_along_axis(example_of, segments, axis=1)
    ids = rows_of(jnp.concatenate([segments, slot], axis=0)[None], ATTN)
    seg_rows = ids[:, :row_count].reshape(ATTN * row_count, length)
    slot_rows = ids[:, row_count:].reshape(ATTN * row_count, length)
    key_slots = jnp.broadcast_to(
        (jnp.arange(examples * patch_count // row_count, dtype=jnp.int32) // patch_count),
        (ATTN * row_count, 1, examples * patch_count // row_count),
    )
    self_ids = (seg_rows[:, :, None], seg_rows[:, None, :])
    cross_ids = (slot_rows[:, :, None], key_slots)

    start = inputs.astype(F32)
    _, scale_self = rms(start, gain_first)
    normed_self, _ = rms(start_rows.astype(F32), gain_first)
    qkv = dot(normed_self, w_self[:, : 3 * hw], 1, 0).astype(BF)
    self_args = ((qkv, 0, hw), (qkv, 1, hw), (qkv, 2, hw))
    mixed_self = attend(True, *self_ids, *self_args)
    after_self = start + reduce_rows(dot(mixed_self, w_self[:, 3 * hw :], 1, 1), ATTN)
    normed, scale_cross = rms(after_self, gain_second)
    normed, shard_ffn = tie(normed, shard_ffn)
    normed_cross = rows_of(normed, ATTN)
    w_ffn = over_planes(shard_ffn, FFN)
    fw = w_ffn.shape[1] // 3
    w_gu, w_dn = w_ffn[:, : 2 * fw], w_ffn[:, 2 * fw :]
    kv = dot(memory, w_cross[:, hw : 3 * hw], 1, 0).astype(BF)
    q = dot(normed_cross, w_cross[:, :hw], 1, 0).astype(BF)
    cross_args = ((q, 0, hw), (kv, 0, hw), (kv, 1, hw))
    mixed_cross = attend(False, *cross_ids, *cross_args)
    after_cross = after_self + reduce_rows(dot(mixed_cross, w_cross[:, 3 * hw :], 1, 1), ATTN)
    normed, scale_ffn = rms(after_cross, gain_third)
    normed_ffn = rows_of(normed, FFN)
    gu = dot(normed_ffn, w_gu, 1, 0)
    gate, up = gu[:, :fw], gu[:, fw:]
    value, slope = gelu_parts(gate)
    hidden = (value * up).astype(BF)

    term_down = term(grad_rows, hidden)
    grad_hidden = dot(grad_rows, w_dn, 1, 0)
    grad_gu = jnp.concatenate(
        [(grad_hidden * up * slope).astype(BF), (grad_hidden * value).astype(BF)], axis=1
    )
    term_gu = term(normed_ffn, grad_gu)
    grad_gu, term_down, term_gu = tie(grad_gu, term_down, term_gu)
    (grad_w_down,) = scatter_weights(term_down, [fw], FFN)
    grad_w_gate, grad_w_up = scatter_weights(term_gu, [fw, fw], FFN)
    grad_normed = reduce_rows(dot(grad_gu, w_gu, 1, 1), FFN)
    grad, gain_grad_ffn = rms_back(after_cross, scale_ffn, gain_third, grad_normed)
    grad_after_cross = grad_out.astype(F32) + grad
    branch = rows_of(grad_after_cross.astype(BF), ATTN)
    branch, hidden = tie(branch, hidden)
    output = after_cross + reduce_rows(dot(hidden, w_dn, 1, 1), FFN)
    term_o = term(branch, mixed_cross)
    grad_mixed = dot(branch, w_cross[:, 3 * hw :], 1, 0).astype(BF)
    grad_q, grad_kv = attend_back(False, *cross_ids, *cross_args, grad_mixed)
    term_q = term(normed_cross, grad_q)
    term_kv = term(memory, grad_kv)
    grad_normed = reduce_rows(dot(grad_q, w_cross[:, :hw], 1, 1), ATTN)
    grad_wq_cross, grad_wk_cross, grad_wv_cross, grad_wo_cross = scatter_weights(
        jnp.concatenate([term_q, term_kv, term_o], axis=1), [hw] * 4, ATTN
    )
    grad, gain_grad_cross = rms_back(after_self, scale_cross, gain_second, grad_normed)
    grad_after_self = grad_after_cross + grad
    branch = rows_of(grad_after_self.astype(BF), ATTN)
    branch, grad_kv = tie(branch, grad_kv)
    grad_memory = reduce_rows(dot(grad_kv, w_cross[:, hw : 3 * hw], 1, 1), ATTN)
    grad_patches = grad_memory.reshape(patches.shape)
    term_o = term(branch, mixed_self)
    grad_mixed = dot(branch, w_self[:, 3 * hw :], 1, 0).astype(BF)
    grad_q, grad_kv = attend_back(True, *self_ids, *self_args, grad_mixed)
    grad_qkv = jnp.concatenate([grad_q, grad_kv], axis=1)
    term_qkv = term(normed_self, grad_qkv)
    term_self = jnp.concatenate([term_qkv, term_o], axis=1)
    grad_qkv, term_self = tie(grad_qkv, term_self)
    term_self = lax.all_to_all(
        term_self.reshape(-1, ATTN, part, 4 * hw),
        "dp",
        1,
        1,
        axis_index_groups=[[m + ATTN * i for m in range(ATTN)] for i in range(dp // ATTN)],
        tiled=True,
    )
    term_self = plane_sum(term_self.reshape(width, -1), ATTN).reshape(ATTN, part, -1)
    grad_wq_self, grad_wk_self, grad_wv_self, grad_wo_self = split(term_self, [hw] * 4)
    grad_normed = reduce_rows(dot(grad_qkv, w_self[:, : 3 * hw], 1, 1), ATTN)
    grad, gain_grad_self = rms_back(start, scale_self, gain_first, grad_normed)
    grad_inputs = grad_after_self + grad

    gain_grads = jnp.concatenate([gain_grad_self, gain_grad_cross, gain_grad_ffn], axis=0)
    bit = 1
    while bit < dp:
        gain_grads = gain_grads + swap(gain_grads, bit)
        bit *= 2
    held = lax.dynamic_slice_in_dim(gain_grads, place * part, part, axis=1)

    return (
        output,
        grad_inputs,
        grad_patches,
        held[0],
        grad_wq_self,
        grad_wk_self,
        grad_wv_self,
        grad_wo_self.T,
        held[1],
        grad_wq_cross,
        grad_wk_cross,
        grad_wv_cross,
        grad_wo_cross.T,
        held[2],
        grad_w_gate,
        grad_w_up,
        grad_w_down.T,
    )


def solution(mesh):
    rows, cut, turned, gain = P("dp", None), P("dp", "mp"), P("mp", "dp"), P("dp")
    attention = (gain, cut, cut, cut, turned)
    weights = attention + attention + (gain, cut, cut, turned)
    return jax.shard_map(
        on_device,
        mesh=mesh,
        in_specs=(rows, rows, rows, P("dp", None, None), rows) + weights,
        out_specs=(rows, rows, P("dp", None, None)) + weights,
        check_vma=False,
    )
```

```python
import functools

import jax
import jax.numpy as jnp
from jax import lax
from jax.experimental.layout import Layout, with_layout_constraint
from jax.experimental import pallas as pl
from jax.experimental.pallas import tpu as pltpu
from jax.sharding import PartitionSpec as P

HEAD_DIM = 64
ATTN = 4
FFN = 4
EPS = 1e-06
NEG = -1e30
BF = jnp.bfloat16
F32 = jnp.float32


def dot(a, b, da, db):
    return lax.dot_general(a, b, (((da,), (db,)), ((), ())), preferred_element_type=F32)


def mask_of(qid_ref, kid_ref, causal):
    allowed = qid_ref[...] == kid_ref[...]
    if causal:
        rows = lax.broadcasted_iota(jnp.int32, allowed.shape, 0)
        cols = lax.broadcasted_iota(jnp.int32, allowed.shape, 1)
        allowed = allowed & (rows >= cols)
    return allowed


def soft(scores, allowed):
    scores = jnp.where(allowed, scores * HEAD_DIM ** (-0.5), NEG)
    raised = jnp.exp(scores - jnp.max(scores, axis=-1, keepdims=True))
    return raised * (1.0 / jnp.sum(raised, axis=-1, keepdims=True))


def heads_of(ref):
    return [ref[:, first : first + HEAD_DIM] for first in range(0, ref.shape[1], HEAD_DIM)]


def attend_kernel(causal, qid_ref, kid_ref, q_ref, k_ref, v_ref, out_ref):
    allowed = mask_of(qid_ref, kid_ref, causal)
    scores = jnp.stack([dot(q, k, 1, 1) for q, k in zip(heads_of(q_ref), heads_of(k_ref))])
    probs = soft(scores, allowed[None]).astype(BF)
    pieces = [dot(probs[h], v, 1, 0).astype(BF) for h, v in enumerate(heads_of(v_ref))]
    out_ref[...] = jnp.concatenate(pieces, axis=1)


def attend_back_kernel(causal, qid_ref, kid_ref, q_ref, k_ref, v_ref, g_ref, dq_ref, dkv_ref):
    allowed = mask_of(qid_ref, kid_ref, causal)
    scale = HEAD_DIM ** (-0.5)
    qs, ks, vs, gs = heads_of(q_ref), heads_of(k_ref), heads_of(v_ref), heads_of(g_ref)
    scores = jnp.stack([dot(q, k, 1, 1) for q, k in zip(qs, ks)])
    grad_probs = jnp.stack([dot(g, v, 1, 1) for g, v in zip(gs, vs)])
    probs = soft(scores, allowed[None])
    centre = jnp.sum(probs * grad_probs, axis=-1, keepdims=True)
    ds = (probs * (grad_probs - centre)).astype(BF)
    probs = probs.astype(BF)
    dvs = [dot(probs[h], g, 0, 0).astype(BF) for h, g in enumerate(gs)]
    dqs = [(dot(ds[h], k, 1, 0) * scale).astype(BF) for h, k in enumerate(ks)]
    dks = [(dot(ds[h], q, 0, 0) * scale).astype(BF) for h, q in enumerate(qs)]
    dq_ref[...] = jnp.concatenate(dqs, axis=1)
    dkv_ref[...] = jnp.concatenate(dks + dvs, axis=1)


def id_specs(length, keys):
    return [
        pl.BlockSpec((None, length, 1), lambda r: (r, 0, 0)),
        pl.BlockSpec((None, 1, keys), lambda r: (r, 0, 0)),
    ]


def attend(causal, qid, kid, q, k, v):
    rows, length, _ = qid.shape
    keys = kid.shape[2]
    width = q[2]
    specs = [
        pl.BlockSpec((n, width), functools.partial(lambda c, r: (r, c), col))
        for n, col in ((length, q[1]), (keys, k[1]), (keys, v[1]))
    ]
    return pl.pallas_call(
        functools.partial(attend_kernel, causal),
        grid=(rows,),
        in_specs=id_specs(length, keys) + specs,
        out_specs=pl.BlockSpec((length, width), lambda r: (r, 0)),
        out_shape=jax.ShapeDtypeStruct((rows * length, width), BF),
        cost_estimate=pl.CostEstimate(
            flops=4 * rows * length * keys * width,
            transcendentals=rows * length * keys * width // HEAD_DIM,
            bytes_accessed=8 * rows * length * width,
        ),
    )(qid, kid, q[0], k[0], v[0])


def attend_back(causal, qid, kid, q, k, v, g):
    rows, length, _ = qid.shape
    keys = kid.shape[2]
    width = q[2]
    specs = [
        pl.BlockSpec((n, width), functools.partial(lambda c, r: (r, c), col))
        for n, col in ((length, q[1]), (keys, k[1]), (keys, v[1]), (length, 0))
    ]
    return pl.pallas_call(
        functools.partial(attend_back_kernel, causal),
        grid=(rows,),
        in_specs=id_specs(length, keys) + specs,
        out_specs=[
            pl.BlockSpec((length, width), lambda r: (r, 0)),
            pl.BlockSpec((keys, 2 * width), lambda r: (r, 0)),
        ],
        out_shape=[
            jax.ShapeDtypeStruct((rows * length, width), BF),
            jax.ShapeDtypeStruct((rows * keys, 2 * width), BF),
        ],
        cost_estimate=pl.CostEstimate(
            flops=10 * rows * length * keys * width,
            transcendentals=rows * length * keys * width // HEAD_DIM,
            bytes_accessed=14 * rows * length * width,
        ),
    )(qid, kid, q[0], k[0], v[0], g)


def term(source, grad):
    return with_layout_constraint(dot(source, grad, 0, 0).astype(BF), Layout((0, 1)))


def rms(values, gain):
    scale = lax.rsqrt(jnp.mean(values * values, axis=-1, keepdims=True) + EPS)
    return (values * scale * gain).astype(BF), scale


def rms_back(values, scale, gain, grad):
    weighted = grad * gain
    mean = jnp.mean(weighted * values, axis=-1, keepdims=True)
    return (
        scale * weighted - values * (scale * scale * scale) * mean,
        jnp.sum(grad * values * scale, axis=0, keepdims=True),
    )


def gelu_parts(gate):
    c = (2.0 / jnp.pi) ** 0.5
    inner = jnp.tanh(c * (gate + 0.044715 * gate * gate * gate))
    value = 0.5 * gate * (1.0 + inner)
    slope = 0.5 * (1.0 + inner) + 0.5 * gate * (1.0 - inner * inner) * c * (
        1.0 + 3 * 0.044715 * gate * gate
    )
    return value, slope


def on_device(
    inputs,
    segments,
    example_of,
    patches,
    grad_out,
    gain_self,
    wq_self,
    wk_self,
    wv_self,
    wo_self,
    gain_cross,
    wq_cross,
    wk_cross,
    wv_cross,
    wo_cross,
    gain_ffn,
    w_gate,
    w_up,
    w_down,
):
    dp = lax.axis_size("dp")
    place = lax.axis_index("dp")
    tokens, width = inputs.shape
    part = width // dp

    def tie(*values):
        return lax.optimization_barrier(values)

    def swap(value, distance):
        return lax.ppermute(value, "dp", [(i, i ^ distance) for i in range(dp)])

    def swap_mp(value):
        return lax.ppermute(value, "mp", [(0, 1), (1, 0)])

    def planes(inner):
        return [[m + inner * i for i in range(dp // inner)] for m in range(inner)]

    def rows_of(value, inner):
        even = [value] + [swap(value, d) for d in range(2, inner, 2)]
        odd = swap(jnp.stack(even), 1)
        return jnp.concatenate(
            [odd[d // 2] if d % 2 else even[d // 2] for d in range(inner)], axis=0
        )

    def reduce_rows(partial, inner):
        parts = partial.astype(BF).reshape(inner, -1, partial.shape[1])
        near = swap(jnp.stack([parts[d] for d in range(1, inner, 2)]), 1)
        total = parts[0].astype(F32) + near[0].astype(F32)
        for d in range(2, inner, 2):
            term = (parts[d].astype(F32) + near[d // 2].astype(F32)).astype(BF)
            total = total + swap(term, d).astype(F32)
        total = total.astype(BF)
        return total.astype(F32) + swap_mp(total).astype(F32)

    def exchange(blocks, inner):
        groups = [[m + inner * i for m in range(inner)] for i in range(dp // inner)]
        return lax.all_to_all(blocks, "dp", 0, 0, axis_index_groups=groups, tiled=True)

    def pack(weights, inner):
        return jnp.stack(
            [
                jnp.concatenate(
                    [
                        w[:, i * (w.shape[1] // inner) : (i + 1) * (w.shape[1] // inner)]
                        for w in weights
                    ],
                    axis=1,
                )
                for i in range(inner)
            ]
        )

    def over_planes(shard, inner):
        shard = shard.reshape(inner * part, -1)
        return lax.all_gather(shard, "dp", axis_index_groups=planes(inner), tiled=True)

    def ring_start(weights):
        def cut(j):
            pieces = []
            for w in weights:
                columns = w.shape[1] // ATTN
                at = pl.multiple_of(((place % ATTN) ^ j) * columns, columns)
                pieces.append(lax.dynamic_slice_in_dim(w, at, columns, axis=1))
            return jnp.concatenate(pieces, axis=1)

        far = jnp.stack([swap(cut(2), 2), swap(cut(3), 3)])
        return [cut(0)[None], swap(cut(1), 1)[None], far]

    def ring_step(held):
        return [lax.ppermute(h, "dp", [(i, (i + ATTN) % dp) for i in range(dp)]) for h in held]

    def placed(kept):
        mine, plane, outer = place % ATTN, place // ATTN, dp // ATTN
        full = jnp.zeros((width, kept[0][0].shape[2]), BF)
        for step, held in enumerate(kept):
            for h, js in zip(held, ((0,), (1,), (2, 3))):
                for n, j in enumerate(js):
                    at = (((plane - step) % outer) * ATTN + (mine ^ j)) * part
                    full = lax.dynamic_update_slice(full, h[n], (at, 0))
        return full

    def plane_sum(whole, inner):
        return lax.psum_scatter(whole, "dp", axis_index_groups=planes(inner), tiled=True)

    def split(pieces, widths):
        out, at = [], 0
        for w in widths:
            cut = slice(at, at + w)
            out.append(jnp.concatenate([x[:, cut] for x in pieces], axis=1).astype(F32))
            at += w
        return out

    def scatter_weights(whole, widths, inner):
        held = plane_sum(whole, inner).reshape(inner, part, -1)
        return split(exchange(held, inner), widths)

    first = [wq_self, wk_self, wv_self, wo_self.T]
    ring = dp // ATTN == 4
    packed_cross = pack([wq_cross, wk_cross, wv_cross, wo_cross.T], ATTN)
    if ring:
        kept = [ring_start(first)]
        kept.append(ring_step(kept[0]))
        kept[1][2], inputs, packed_cross = tie(kept[1][2], inputs, packed_cross)
        kept.append(ring_step(kept[1]))
        kept[2][2], gain_self, segments = tie(kept[2][2], gain_self, segments)
        kept.append(ring_step(kept[2]))
    else:
        shard_self = exchange(pack(first, ATTN), ATTN)
        shard_self, inputs, packed_cross = tie(shard_self, inputs, packed_cross)
        w_self = over_planes(shard_self, ATTN)
    start_rows = rows_of(inputs, ATTN)
    shard_cross = exchange(packed_cross, ATTN)
    packed_ffn = pack([w_gate, w_up, w_down.T], FFN)
    patch_rows = patches.reshape(-1, width)
    if ring:
        kept[3][2], shard_cross, start_rows, patch_rows, packed_ffn, grad_out = tie(
            kept[3][2], shard_cross, start_rows, patch_rows, packed_ffn, grad_out
        )
        w_self = placed(kept)
    w_cross = over_planes(shard_cross, ATTN)
    memory = rows_of(patch_rows, ATTN)
    shard_ffn = exchange(packed_ffn, FFN)
    shard_ffn, grad_out, memory = tie(shard_ffn, grad_out, memory)
    grad_rows = rows_of(grad_out, FFN)
    hw = w_self.shape[1] // 4

    gains = jnp.stack([gain_self, gain_cross, gain_ffn]).astype(F32)
    held = rows_of(jnp.stack([gains] + [swap(gains, d) for d in range(ATTN, dp, ATTN)])[None], ATTN)
    all_gains = jnp.zeros((dp, 3, part), F32)
    for i in range(dp // ATTN):
        for j in range(ATTN):
            all_gains = lax.dynamic_update_slice(
                all_gains, held[j, i][None], (place ^ (i * ATTN + j), 0, 0)
            )
    gain_first, gain_second, gain_third = (all_gains[:, i].reshape(1, width) for i in range(3))

    row_count, length = segments.shape
    examples, patch_count, _ = patches.shape
    slot = jnp.take_along_axis(example_of, segments, axis=1)
    ids = rows_of(jnp.concatenate([segments, slot], axis=0)[None], ATTN)
    seg_rows = ids[:, :row_count].reshape(ATTN * row_count, length)
    slot_rows = ids[:, row_count:].reshape(ATTN * row_count, length)
    key_slots = jnp.broadcast_to(
        (jnp.arange(examples * patch_count // row_count, dtype=jnp.int32) // patch_count),
        (ATTN * row_count, 1, examples * patch_count // row_count),
    )
    self_ids = (seg_rows[:, :, None], seg_rows[:, None, :])
    cross_ids = (slot_rows[:, :, None], key_slots)

    start = inputs.astype(F32)
    _, scale_self = rms(start, gain_first)
    normed_self, _ = rms(start_rows.astype(F32), gain_first)
    qkv = dot(normed_self, w_self[:, : 3 * hw], 1, 0).astype(BF)
    self_args = ((qkv, 0, hw), (qkv, 1, hw), (qkv, 2, hw))
    mixed_self = attend(True, *self_ids, *self_args)
    after_self = start + reduce_rows(dot(mixed_self, w_self[:, 3 * hw :], 1, 1), ATTN)
    normed, scale_cross = rms(after_self, gain_second)
    normed, shard_ffn = tie(normed, shard_ffn)
    normed_cross = rows_of(normed, ATTN)
    w_ffn = over_planes(shard_ffn, FFN)
    fw = w_ffn.shape[1] // 3
    w_gu, w_dn = w_ffn[:, : 2 * fw], w_ffn[:, 2 * fw :]
    kv = dot(memory, w_cross[:, hw : 3 * hw], 1, 0).astype(BF)
    q = dot(normed_cross, w_cross[:, :hw], 1, 0).astype(BF)
    cross_args = ((q, 0, hw), (kv, 0, hw), (kv, 1, hw))
    mixed_cross = attend(False, *cross_ids, *cross_args)
    after_cross = after_self + reduce_rows(dot(mixed_cross, w_cross[:, 3 * hw :], 1, 1), ATTN)
    normed, scale_ffn = rms(after_cross, gain_third)
    normed_ffn = rows_of(normed, FFN)
    gu = dot(normed_ffn, w_gu, 1, 0)
    gate, up = gu[:, :fw], gu[:, fw:]
    value, slope = gelu_parts(gate)
    hidden = (value * up).astype(BF)

    term_down = term(grad_rows, hidden)
    term_down, grad_rows = tie(term_down, grad_rows)
    grad_hidden = dot(grad_rows, w_dn, 1, 0)
    grad_gu = jnp.concatenate(
        [(grad_hidden * up * slope).astype(BF), (grad_hidden * value).astype(BF)], axis=1
    )
    term_gu = term(normed_ffn, grad_gu)
    grad_gu, term_gu = tie(grad_gu, term_gu)
    (grad_w_down,) = scatter_weights(term_down, [fw], FFN)
    grad_w_gate, grad_w_up = scatter_weights(term_gu, [fw, fw], FFN)
    grad_normed = reduce_rows(dot(grad_gu, w_gu, 1, 1), FFN)
    grad, gain_grad_ffn = rms_back(after_cross, scale_ffn, gain_third, grad_normed)
    grad_after_cross = grad_out.astype(F32) + grad
    branch = rows_of(grad_after_cross.astype(BF), ATTN)
    branch, hidden = tie(branch, hidden)
    output = after_cross + reduce_rows(dot(hidden, w_dn, 1, 1), FFN)
    term_o = term(branch, mixed_cross)
    grad_mixed = dot(branch, w_cross[:, 3 * hw :], 1, 0).astype(BF)
    grad_q, grad_kv = attend_back(False, *cross_ids, *cross_args, grad_mixed)
    term_q = term(normed_cross, grad_q)
    term_kv = term(memory, grad_kv)
    grad_normed = reduce_rows(dot(grad_q, w_cross[:, :hw], 1, 1), ATTN)
    grad_wq_cross, grad_wk_cross, grad_wv_cross, grad_wo_cross = scatter_weights(
        jnp.concatenate([term_q, term_kv, term_o], axis=1), [hw] * 4, ATTN
    )
    grad, gain_grad_cross = rms_back(after_self, scale_cross, gain_second, grad_normed)
    grad_after_self = grad_after_cross + grad
    branch = rows_of(grad_after_self.astype(BF), ATTN)
    branch, grad_kv = tie(branch, grad_kv)
    grad_memory = reduce_rows(dot(grad_kv, w_cross[:, hw : 3 * hw], 1, 1), ATTN)
    grad_patches = grad_memory.reshape(patches.shape)
    term_o = term(branch, mixed_self)
    grad_mixed = dot(branch, w_self[:, 3 * hw :], 1, 0).astype(BF)
    grad_q, grad_kv = attend_back(True, *self_ids, *self_args, grad_mixed)
    grad_qkv = jnp.concatenate([grad_q, grad_kv], axis=1)
    term_qkv = term(normed_self, grad_qkv)
    term_self = jnp.concatenate([term_qkv, term_o], axis=1)
    grad_qkv, term_self = tie(grad_qkv, term_self)
    term_self = lax.all_to_all(
        term_self.reshape(-1, ATTN, part, 4 * hw),
        "dp",
        1,
        1,
        axis_index_groups=[[m + ATTN * i for m in range(ATTN)] for i in range(dp // ATTN)],
        tiled=True,
    )
    term_self = plane_sum(term_self.reshape(width, -1), ATTN).reshape(ATTN, part, -1)
    grad_wq_self, grad_wk_self, grad_wv_self, grad_wo_self = split(term_self, [hw] * 4)
    grad_normed = reduce_rows(dot(grad_qkv, w_self[:, : 3 * hw], 1, 1), ATTN)
    grad, gain_grad_self = rms_back(start, scale_self, gain_first, grad_normed)
    grad_inputs = grad_after_self + grad

    gain_grads = jnp.concatenate([gain_grad_self, gain_grad_cross, gain_grad_ffn], axis=0)
    bit = 1
    while bit < dp:
        gain_grads = gain_grads + swap(gain_grads, bit)
        bit *= 2
    held = lax.dynamic_slice_in_dim(gain_grads, place * part, part, axis=1)

    return (
        output,
        grad_inputs,
        grad_patches,
        held[0],
        grad_wq_self,
        grad_wk_self,
        grad_wv_self,
        grad_wo_self.T,
        held[1],
        grad_wq_cross,
        grad_wk_cross,
        grad_wv_cross,
        grad_wo_cross.T,
        held[2],
        grad_w_gate,
        grad_w_up,
        grad_w_down.T,
    )


def solution(mesh):
    rows, cut, turned, gain = P("dp", None), P("dp", "mp"), P("mp", "dp"), P("dp")
    attention = (gain, cut, cut, cut, turned)
    weights = attention + attention + (gain, cut, cut, turned)
    return jax.shard_map(
        on_device,
        mesh=mesh,
        in_specs=(rows, rows, rows, P("dp", None, None), rows) + weights,
        out_specs=(rows, rows, P("dp", None, None)) + weights,
        check_vma=False,
    )
```

```python
import functools

import jax
import jax.numpy as jnp
from jax import lax
from jax.experimental.layout import Layout, with_layout_constraint
from jax.experimental import pallas as pl
from jax.experimental.pallas import tpu as pltpu
from jax.sharding import PartitionSpec as P

HEAD_DIM = 64
ATTN = 4
FFN = 4
EPS = 1e-06
NEG = -1e30
BF = jnp.bfloat16
F32 = jnp.float32


def dot(a, b, da, db):
    return lax.dot_general(a, b, (((da,), (db,)), ((), ())), preferred_element_type=F32)


def mask_of(qid_ref, kid_ref, causal):
    allowed = qid_ref[...] == kid_ref[...]
    if causal:
        rows = lax.broadcasted_iota(jnp.int32, allowed.shape, 0)
        cols = lax.broadcasted_iota(jnp.int32, allowed.shape, 1)
        allowed = allowed & (rows >= cols)
    return allowed


def soft(scores, allowed):
    scores = jnp.where(allowed, scores * HEAD_DIM ** (-0.5), NEG)
    raised = jnp.exp(scores - jnp.max(scores, axis=-1, keepdims=True))
    return raised * (1.0 / jnp.sum(raised, axis=-1, keepdims=True))


def heads_of(ref):
    return [ref[:, first : first + HEAD_DIM] for first in range(0, ref.shape[1], HEAD_DIM)]


def attend_kernel(causal, qid_ref, kid_ref, q_ref, k_ref, v_ref, out_ref):
    allowed = mask_of(qid_ref, kid_ref, causal)
    scores = jnp.stack([dot(q, k, 1, 1) for q, k in zip(heads_of(q_ref), heads_of(k_ref))])
    probs = soft(scores, allowed[None]).astype(BF)
    pieces = [dot(probs[h], v, 1, 0).astype(BF) for h, v in enumerate(heads_of(v_ref))]
    out_ref[...] = jnp.concatenate(pieces, axis=1)


def attend_back_kernel(causal, qid_ref, kid_ref, q_ref, k_ref, v_ref, g_ref, dq_ref, dkv_ref):
    allowed = mask_of(qid_ref, kid_ref, causal)
    scale = HEAD_DIM ** (-0.5)
    qs, ks, vs, gs = heads_of(q_ref), heads_of(k_ref), heads_of(v_ref), heads_of(g_ref)
    scores = jnp.stack([dot(q, k, 1, 1) for q, k in zip(qs, ks)])
    grad_probs = jnp.stack([dot(g, v, 1, 1) for g, v in zip(gs, vs)])
    probs = soft(scores, allowed[None])
    centre = jnp.sum(probs * grad_probs, axis=-1, keepdims=True)
    ds = (probs * (grad_probs - centre)).astype(BF)
    probs = probs.astype(BF)
    dvs = [dot(probs[h], g, 0, 0).astype(BF) for h, g in enumerate(gs)]
    dqs = [(dot(ds[h], k, 1, 0) * scale).astype(BF) for h, k in enumerate(ks)]
    dks = [(dot(ds[h], q, 0, 0) * scale).astype(BF) for h, q in enumerate(qs)]
    dq_ref[...] = jnp.concatenate(dqs, axis=1)
    dkv_ref[...] = jnp.concatenate(dks + dvs, axis=1)


def id_specs(length, keys):
    return [
        pl.BlockSpec((None, length, 1), lambda r: (r, 0, 0)),
        pl.BlockSpec((None, 1, keys), lambda r: (r, 0, 0)),
    ]


def attend(causal, qid, kid, q, k, v):
    rows, length, _ = qid.shape
    keys = kid.shape[2]
    width = q[2]
    specs = [
        pl.BlockSpec((n, width), functools.partial(lambda c, r: (r, c), col))
        for n, col in ((length, q[1]), (keys, k[1]), (keys, v[1]))
    ]
    return pl.pallas_call(
        functools.partial(attend_kernel, causal),
        grid=(rows,),
        in_specs=id_specs(length, keys) + specs,
        out_specs=pl.BlockSpec((length, width), lambda r: (r, 0)),
        out_shape=jax.ShapeDtypeStruct((rows * length, width), BF),
        cost_estimate=pl.CostEstimate(
            flops=4 * rows * length * keys * width,
            transcendentals=rows * length * keys * width // HEAD_DIM,
            bytes_accessed=8 * rows * length * width,
        ),
    )(qid, kid, q[0], k[0], v[0])


def attend_back(causal, qid, kid, q, k, v, g):
    rows, length, _ = qid.shape
    keys = kid.shape[2]
    width = q[2]
    specs = [
        pl.BlockSpec((n, width), functools.partial(lambda c, r: (r, c), col))
        for n, col in ((length, q[1]), (keys, k[1]), (keys, v[1]), (length, 0))
    ]
    return pl.pallas_call(
        functools.partial(attend_back_kernel, causal),
        grid=(rows,),
        in_specs=id_specs(length, keys) + specs,
        out_specs=[
            pl.BlockSpec((length, width), lambda r: (r, 0)),
            pl.BlockSpec((keys, 2 * width), lambda r: (r, 0)),
        ],
        out_shape=[
            jax.ShapeDtypeStruct((rows * length, width), BF),
            jax.ShapeDtypeStruct((rows * keys, 2 * width), BF),
        ],
        cost_estimate=pl.CostEstimate(
            flops=10 * rows * length * keys * width,
            transcendentals=rows * length * keys * width // HEAD_DIM,
            bytes_accessed=14 * rows * length * width,
        ),
    )(qid, kid, q[0], k[0], v[0], g)


def term(source, grad):
    return with_layout_constraint(dot(source, grad, 0, 0).astype(BF), Layout((0, 1)))


def rms(values, gain):
    scale = lax.rsqrt(jnp.mean(values * values, axis=-1, keepdims=True) + EPS)
    return (values * scale * gain).astype(BF), scale


def rms_back(values, scale, gain, grad):
    weighted = grad * gain
    mean = jnp.mean(weighted * values, axis=-1, keepdims=True)
    return (
        scale * weighted - values * (scale * scale * scale) * mean,
        jnp.sum(grad * values * scale, axis=0, keepdims=True),
    )


def gelu_parts(gate):
    c = (2.0 / jnp.pi) ** 0.5
    inner = jnp.tanh(c * (gate + 0.044715 * gate * gate * gate))
    value = 0.5 * gate * (1.0 + inner)
    slope = 0.5 * (1.0 + inner) + 0.5 * gate * (1.0 - inner * inner) * c * (
        1.0 + 3 * 0.044715 * gate * gate
    )
    return value, slope


def on_device(
    inputs,
    segments,
    example_of,
    patches,
    grad_out,
    gain_self,
    wq_self,
    wk_self,
    wv_self,
    wo_self,
    gain_cross,
    wq_cross,
    wk_cross,
    wv_cross,
    wo_cross,
    gain_ffn,
    w_gate,
    w_up,
    w_down,
):
    dp = lax.axis_size("dp")
    place = lax.axis_index("dp")
    tokens, width = inputs.shape
    part = width // dp

    def tie(*values):
        return lax.optimization_barrier(values)

    def swap(value, distance):
        return lax.ppermute(value, "dp", [(i, i ^ distance) for i in range(dp)])

    def swap_mp(value):
        return lax.ppermute(value, "mp", [(0, 1), (1, 0)])

    def planes(inner):
        return [[m + inner * i for i in range(dp // inner)] for m in range(inner)]

    def rows_of(value, inner):
        even = [value] + [swap(value, d) for d in range(2, inner, 2)]
        odd = swap(jnp.stack(even), 1)
        return jnp.concatenate(
            [odd[d // 2] if d % 2 else even[d // 2] for d in range(inner)], axis=0
        )

    def reduce_rows(partial, inner):
        parts = partial.astype(BF).reshape(inner, -1, partial.shape[1])
        near = swap(jnp.stack([parts[d] for d in range(1, inner, 2)]), 1)
        total = parts[0].astype(F32) + near[0].astype(F32)
        for d in range(2, inner, 2):
            term = (parts[d].astype(F32) + near[d // 2].astype(F32)).astype(BF)
            total = total + swap(term, d).astype(F32)
        total = total.astype(BF)
        return total.astype(F32) + swap_mp(total).astype(F32)

    def exchange(blocks, inner):
        groups = [[m + inner * i for m in range(inner)] for i in range(dp // inner)]
        return lax.all_to_all(blocks, "dp", 0, 0, axis_index_groups=groups, tiled=True)

    def pack(weights, inner):
        return jnp.stack(
            [
                jnp.concatenate(
                    [
                        w[:, i * (w.shape[1] // inner) : (i + 1) * (w.shape[1] // inner)]
                        for w in weights
                    ],
                    axis=1,
                )
                for i in range(inner)
            ]
        )

    def over_planes(shard, inner):
        shard = shard.reshape(inner * part, -1)
        return lax.all_gather(shard, "dp", axis_index_groups=planes(inner), tiled=True)

    def ring_start(weights):
        def cut(j):
            pieces = []
            for w in weights:
                columns = w.shape[1] // ATTN
                at = pl.multiple_of(((place % ATTN) ^ j) * columns, columns)
                pieces.append(lax.dynamic_slice_in_dim(w, at, columns, axis=1))
            return jnp.concatenate(pieces, axis=1)

        far = jnp.stack([swap(cut(2), 2), swap(cut(3), 3)])
        return [cut(0)[None], swap(cut(1), 1)[None], far]

    def ring_step(held):
        return [lax.ppermute(h, "dp", [(i, (i + ATTN) % dp) for i in range(dp)]) for h in held]

    def placed(kept):
        mine, plane, outer = place % ATTN, place // ATTN, dp // ATTN
        full = jnp.zeros((width, kept[0][0].shape[2]), BF)
        for step, held in enumerate(kept):
            for h, js in zip(held, ((0,), (1,), (2, 3))):
                for n, j in enumerate(js):
                    at = (((plane - step) % outer) * ATTN + (mine ^ j)) * part
                    full = lax.dynamic_update_slice(full, h[n], (at, 0))
        return full

    def plane_sum(whole, inner):
        return lax.psum_scatter(whole, "dp", axis_index_groups=planes(inner), tiled=True)

    def split(pieces, widths):
        out, at = [], 0
        for w in widths:
            cut = slice(at, at + w)
            out.append(jnp.concatenate([x[:, cut] for x in pieces], axis=1).astype(F32))
            at += w
        return out

    def scatter_weights(whole, widths, inner):
        held = plane_sum(whole, inner).reshape(inner, part, -1)
        return split(exchange(held, inner), widths)

    first = [wq_self, wk_self, wv_self, wo_self.T]
    ring = dp // ATTN == 4
    packed_cross = pack([wq_cross, wk_cross, wv_cross, wo_cross.T], ATTN)
    if ring:
        kept = [ring_start(first)]
        kept.append(ring_step(kept[0]))
        kept[1][2], inputs, packed_cross = tie(kept[1][2], inputs, packed_cross)
        kept.append(ring_step(kept[1]))
        kept.append(ring_step(kept[2]))
    else:
        shard_self = exchange(pack(first, ATTN), ATTN)
        shard_self, inputs, packed_cross = tie(shard_self, inputs, packed_cross)
        w_self = over_planes(shard_self, ATTN)
    start_rows = rows_of(inputs, ATTN)
    shard_cross = exchange(packed_cross, ATTN)
    packed_ffn = pack([w_gate, w_up, w_down.T], FFN)
    patch_rows = patches.reshape(-1, width)
    if ring:
        kept[3][2], shard_cross, start_rows, patch_rows, packed_ffn, grad_out = tie(
            kept[3][2], shard_cross, start_rows, patch_rows, packed_ffn, grad_out
        )
        kept[3][2], gain_self, segments = tie(kept[3][2], gain_self, segments)
        w_self = placed(kept)
    w_cross = over_planes(shard_cross, ATTN)
    memory = rows_of(patch_rows, ATTN)
    shard_ffn = exchange(packed_ffn, FFN)
    shard_ffn, grad_out, memory = tie(shard_ffn, grad_out, memory)
    grad_rows = rows_of(grad_out, FFN)
    hw = w_self.shape[1] // 4

    gains = jnp.stack([gain_self, gain_cross, gain_ffn]).astype(F32)
    held = rows_of(jnp.stack([gains] + [swap(gains, d) for d in range(ATTN, dp, ATTN)])[None], ATTN)
    all_gains = jnp.zeros((dp, 3, part), F32)
    for i in range(dp // ATTN):
        for j in range(ATTN):
            all_gains = lax.dynamic_update_slice(
                all_gains, held[j, i][None], (place ^ (i * ATTN + j), 0, 0)
            )
    gain_first, gain_second, gain_third = (all_gains[:, i].reshape(1, width) for i in range(3))

    row_count, length = segments.shape
    examples, patch_count, _ = patches.shape
    slot = jnp.take_along_axis(example_of, segments, axis=1)
    ids = rows_of(jnp.concatenate([segments, slot], axis=0)[None], ATTN)
    seg_rows = ids[:, :row_count].reshape(ATTN * row_count, length)
    slot_rows = ids[:, row_count:].reshape(ATTN * row_count, length)
    key_slots = jnp.broadcast_to(
        (jnp.arange(examples * patch_count // row_count, dtype=jnp.int32) // patch_count),
        (ATTN * row_count, 1, examples * patch_count // row_count),
    )
    self_ids = (seg_rows[:, :, None], seg_rows[:, None, :])
    cross_ids = (slot_rows[:, :, None], key_slots)

    start = inputs.astype(F32)
    _, scale_self = rms(start, gain_first)
    normed_self, _ = rms(start_rows.astype(F32), gain_first)
    qkv = dot(normed_self, w_self[:, : 3 * hw], 1, 0).astype(BF)
    self_args = ((qkv, 0, hw), (qkv, 1, hw), (qkv, 2, hw))
    mixed_self = attend(True, *self_ids, *self_args)
    after_self = start + reduce_rows(dot(mixed_self, w_self[:, 3 * hw :], 1, 1), ATTN)
    normed, scale_cross = rms(after_self, gain_second)
    normed, shard_ffn = tie(normed, shard_ffn)
    normed_cross = rows_of(normed, ATTN)
    w_ffn = over_planes(shard_ffn, FFN)
    fw = w_ffn.shape[1] // 3
    w_gu, w_dn = w_ffn[:, : 2 * fw], w_ffn[:, 2 * fw :]
    kv = dot(memory, w_cross[:, hw : 3 * hw], 1, 0).astype(BF)
    q = dot(normed_cross, w_cross[:, :hw], 1, 0).astype(BF)
    cross_args = ((q, 0, hw), (kv, 0, hw), (kv, 1, hw))
    mixed_cross = attend(False, *cross_ids, *cross_args)
    after_cross = after_self + reduce_rows(dot(mixed_cross, w_cross[:, 3 * hw :], 1, 1), ATTN)
    normed, scale_ffn = rms(after_cross, gain_third)
    normed_ffn = rows_of(normed, FFN)
    gu = dot(normed_ffn, w_gu, 1, 0)
    gate, up = gu[:, :fw], gu[:, fw:]
    value, slope = gelu_parts(gate)
    hidden = (value * up).astype(BF)

    term_down = term(grad_rows, hidden)
    term_down, grad_rows = tie(term_down, grad_rows)
    grad_hidden = dot(grad_rows, w_dn, 1, 0)
    grad_gu = jnp.concatenate(
        [(grad_hidden * up * slope).astype(BF), (grad_hidden * value).astype(BF)], axis=1
    )
    term_gu = term(normed_ffn, grad_gu)
    grad_gu, term_gu = tie(grad_gu, term_gu)
    (grad_w_down,) = scatter_weights(term_down, [fw], FFN)
    grad_w_gate, grad_w_up = scatter_weights(term_gu, [fw, fw], FFN)
    grad_normed = reduce_rows(dot(grad_gu, w_gu, 1, 1), FFN)
    grad, gain_grad_ffn = rms_back(after_cross, scale_ffn, gain_third, grad_normed)
    grad_after_cross = grad_out.astype(F32) + grad
    branch = rows_of(grad_after_cross.astype(BF), ATTN)
    branch, hidden = tie(branch, hidden)
    output = after_cross + reduce_rows(dot(hidden, w_dn, 1, 1), FFN)
    term_o = term(branch, mixed_cross)
    grad_mixed = dot(branch, w_cross[:, 3 * hw :], 1, 0).astype(BF)
    grad_q, grad_kv = attend_back(False, *cross_ids, *cross_args, grad_mixed)
    term_q = term(normed_cross, grad_q)
    term_kv = term(memory, grad_kv)
    grad_normed = reduce_rows(dot(grad_q, w_cross[:, :hw], 1, 1), ATTN)
    grad_wq_cross, grad_wk_cross, grad_wv_cross, grad_wo_cross = scatter_weights(
        jnp.concatenate([term_q, term_kv, term_o], axis=1), [hw] * 4, ATTN
    )
    grad, gain_grad_cross = rms_back(after_self, scale_cross, gain_second, grad_normed)
    grad_after_self = grad_after_cross + grad
    branch = rows_of(grad_after_self.astype(BF), ATTN)
    branch, grad_kv = tie(branch, grad_kv)
    grad_memory = reduce_rows(dot(grad_kv, w_cross[:, hw : 3 * hw], 1, 1), ATTN)
    grad_patches = grad_memory.reshape(patches.shape)
    term_o = term(branch, mixed_self)
    grad_mixed = dot(branch, w_self[:, 3 * hw :], 1, 0).astype(BF)
    grad_q, grad_kv = attend_back(True, *self_ids, *self_args, grad_mixed)
    grad_qkv = jnp.concatenate([grad_q, grad_kv], axis=1)
    term_qkv = term(normed_self, grad_qkv)
    term_self = jnp.concatenate([term_qkv, term_o], axis=1)
    grad_qkv, term_self = tie(grad_qkv, term_self)
    term_self = lax.all_to_all(
        term_self.reshape(-1, ATTN, part, 4 * hw),
        "dp",
        1,
        1,
        axis_index_groups=[[m + ATTN * i for m in range(ATTN)] for i in range(dp // ATTN)],
        tiled=True,
    )
    term_self = plane_sum(term_self.reshape(width, -1), ATTN).reshape(ATTN, part, -1)
    grad_wq_self, grad_wk_self, grad_wv_self, grad_wo_self = split(term_self, [hw] * 4)
    grad_normed = reduce_rows(dot(grad_qkv, w_self[:, : 3 * hw], 1, 1), ATTN)
    grad, gain_grad_self = rms_back(start, scale_self, gain_first, grad_normed)
    grad_inputs = grad_after_self + grad

    gain_grads = jnp.concatenate([gain_grad_self, gain_grad_cross, gain_grad_ffn], axis=0)
    bit = 1
    while bit < dp:
        gain_grads = gain_grads + swap(gain_grads, bit)
        bit *= 2
    held = lax.dynamic_slice_in_dim(gain_grads, place * part, part, axis=1)

    return (
        output,
        grad_inputs,
        grad_patches,
        held[0],
        grad_wq_self,
        grad_wk_self,
        grad_wv_self,
        grad_wo_self.T,
        held[1],
        grad_wq_cross,
        grad_wk_cross,
        grad_wv_cross,
        grad_wo_cross.T,
        held[2],
        grad_w_gate,
        grad_w_up,
        grad_w_down.T,
    )


def solution(mesh):
    rows, cut, turned, gain = P("dp", None), P("dp", "mp"), P("mp", "dp"), P("dp")
    attention = (gain, cut, cut, cut, turned)
    weights = attention + attention + (gain, cut, cut, turned)
    return jax.shard_map(
        on_device,
        mesh=mesh,
        in_specs=(rows, rows, rows, P("dp", None, None), rows) + weights,
        out_specs=(rows, rows, P("dp", None, None)) + weights,
        check_vma=False,
    )
```
